128 devices in a mesh: flow: 16 (over x, z), cross: 8 (over y, core).
Axes of the slice: x: 4, y: 4, z: 4, core: 2. Of those that a mesh axis runs over, the one named last changes fastest.
Arguments:
- right_side: float32 [16, 512, 320], P('flow', 'cross'), may hold values from -6 to 6
- old_state: float32 [16, 512, 320], P('flow', 'cross'), may hold values from -6 to 6
- block_inverse: bfloat16 [16, 512, 320, 320], P('flow', 'cross'), as said below
- flux_jacobian: float32 [16, 512, 4, 25], P('flow', 'cross'), may hold values from -1.35 to 1.35, as said below
- face_lift: float32 [4, 64, 64], replicated, may hold values from -0.75 to 0.75
- upstream: int32 [16, 512], P('flow', 'cross'), may hold values from 0 to 511, as said below
- downstream: int32 [16, 512], P('flow', 'cross'), may hold values from 0 to 511, as said below
- live_counts: int32 [16, 8], P('flow', 'cross'), may hold values from 32 to 64, as said below
Outputs:
- half_sweep: float32 [16, 512, 320], P('flow', 'cross')
- full_sweep: float32 [16, 512, 320], P('flow', 'cross')
The draws below stay inside these ranges and needn't reach their ends.
Inputs may be any that keep to these rules, and one draw needn't show every extreme that they name: In each layer the upstream slots of an aligned block of 4 slots are a permutation of that same block's slots. downstream[l] is the inverse permutation of upstream[l + 1] (of upstream[0] for the last layer): upstream[l + 1, downstream[l, e]] = e. `live_counts`: slots at or beyond the count in their run hold no element; some run is full. `block_inverse`: each block is the sum of a multiple of the identity and a full dense part. `flux_jacobian`: entries are centred; those of the upstream and downstream faces are of order 0.45, those of the left and right faces of order 0.27.
All inputs are finite; a program needn't handle non-finite values.
Results may differ from the reference program's by a relative error of at most 0.017.
Values sent between devices are 32-bit elements; how exact they have to be, the bound alone decides.
No kernel may reach another device: no remote copies, remote signals or barrier semaphores. Data moves between devices by JAX's collectives and lax.ppermute only.
A program may use at most 64 MiB of HBM per device.

```python
import math
import jax
import jax.numpy as jnp
from jax import lax

NVAR = 5
NB = 64
B = 320
E_DEV = 64
GRP = 4
LAYERS = 16
ELEMS = 512
N_CROSS = 8


def one_shuffle(block_key):
    return jax.random.permutation(block_key, GRP)


def neighbour_lists(key):
    block_total = LAYERS * ELEMS // GRP
    block_keys = jax.random.split(jax.random.fold_in(key, 71), block_total)
    shuffles = jax.vmap(one_shuffle)(block_keys).astype(jnp.int32)
    offsets = jnp.arange(block_total, dtype=jnp.int32) % (ELEMS // GRP) * GRP
    upward = (shuffles + offsets[:, None]).reshape(LAYERS, ELEMS)
    following = jnp.roll(upward, -1, axis=0)
    downward = jnp.argsort(following, axis=1, stable=True).astype(jnp.int32)
    return (upward, downward)


def draw_upstream(key, part):
    return neighbour_lists(key)[0]


def draw_downstream(key, part):
    return neighbour_lists(key)[1]


def draw_live_counts(key, part):
    lowest = max(1, E_DEV // 2)
    drawn = jax.random.randint(jax.random.fold_in(key, 5), (LAYERS, N_CROSS), lowest, E_DEV + 1, dtype=jnp.int32)
    spot_row = jax.random.randint(jax.random.fold_in(key, 6), (), 0, LAYERS, dtype=jnp.int32)
    spot_col = jax.random.randint(jax.random.fold_in(key, 7), (), 0, N_CROSS, dtype=jnp.int32)
    return drawn.at[spot_row, spot_col].set(E_DEV).astype(jnp.int32)


def draw_block_inverse(key, part):
    noise = jax.random.normal(jax.random.fold_in(key, 9), (LAYERS, ELEMS, B, B), jnp.float32)
    blocks = 0.85 * jnp.eye(B, dtype=jnp.float32) + 0.3 / math.sqrt(B) * noise
    return blocks.astype(jnp.bfloat16)


def draw_flux_jacobian(key, part):
    face_scale = jnp.array([1.0, 1.0, 0.6, 0.6], jnp.float32) / math.sqrt(5.0)
    shape = (LAYERS, ELEMS, 4, NVAR * NVAR)
    raw = jnp.clip(jax.random.normal(jax.random.fold_in(key, 11), shape, jnp.float32), -3.0, 3.0)
    return raw * face_scale[:, None]


def shard_levels(key, shape, cuts, least, top_value):
    def one(dim, parts):
        heights = jax.random.uniform(jax.random.fold_in(jax.random.fold_in(key, 6), dim), (parts,), jnp.float32, least / len(cuts), top_value / len(cuts))
        return jnp.repeat(jnp.exp(heights), shape[dim] // parts).reshape((-1,) + (1,) * (len(shape) - dim - 1))

    gain = one(*cuts[0])
    for cut in cuts[1:]:
        gain = gain * one(*cut)
    return gain


def gaussian(key, dims, width, bound, cuts=(), held_as=jnp.bfloat16):
    factor_of = shard_levels(key, dims, cuts, -0.22, 0.18) if cuts else 1.0
    result = jax.random.normal(key, dims, jnp.float32) * width * factor_of
    return jnp.minimum(jnp.maximum(result, -bound), bound).astype(held_as)


def setup_inputs(seed: int = 0) -> dict:
    seeds = jax.random.split(jax.random.key(seed), 9)
    right_side = gaussian(seeds[0], (LAYERS, ELEMS, B), 1.0, 6.0, ((0, 16), (1, 8)), jnp.float32)
    old_state = gaussian(seeds[1], (LAYERS, ELEMS, B), 1.0, 6.0, ((0, 16), (1, 8)), jnp.float32)
    block_inverse = draw_block_inverse(jax.random.fold_in(seeds[8], 71), 0)
    flux_jacobian = draw_flux_jacobian(jax.random.fold_in(seeds[8], 71), 0)
    face_lift = gaussian(seeds[4], (4, NB, NB), NB ** -0.5, 0.75, (), jnp.float32)
    upstream = draw_upstream(jax.random.fold_in(seeds[8], 71), 0)
    downstream = draw_downstream(jax.random.fold_in(seeds[8], 71), 0)
    live_counts = draw_live_counts(jax.random.fold_in(seeds[8], 71), 0)
    return dict(right_side=right_side, old_state=old_state, block_inverse=block_inverse, flux_jacobian=flux_jacobian, face_lift=face_lift, upstream=upstream, downstream=downstream, live_counts=live_counts)


HIGHEST_PRECISION = lax.Precision.HIGHEST


def couple(values, lift, jacobian_face):
    spread = jnp.einsum("...vc,bc->...vb", values, lift, precision=HIGHEST_PRECISION)
    mixing = jacobian_face.reshape(jacobian_face.shape[:-1] + (5, 5))
    return jnp.einsum("...uv,...vb->...ub", mixing, spread, precision=HIGHEST_PRECISION)


def solve_blocks(inverse, residual, live):
    flat = residual.reshape(residual.shape[:-2] + (-1,)).astype(jnp.bfloat16)
    flat = lax.optimization_barrier(flat).astype(jnp.float32)
    solved = jnp.einsum("...ij,...j->...i", inverse.astype(jnp.float32), flat, precision=HIGHEST_PRECISION)
    return (solved * live[..., None]).reshape(residual.shape)


def sideways(field):
    padded = jnp.pad(field, ((0, 0), (1, 1), (0, 0), (0, 0)))
    return padded[:, :-2], padded[:, 2:]


def reference(right_side, old_state, block_inverse, flux_jacobian, face_lift, upstream, downstream, live_counts):
    layer_count, elem_count, unknowns = right_side.shape
    grid_shape = (layer_count, elem_count, 5, unknowns // 5)
    source = right_side.reshape(grid_shape)
    slot_index = jnp.arange(elem_count, dtype=jnp.int32)
    owner_counts = live_counts[:, slot_index // E_DEV]
    live = (slot_index[None, :] % E_DEV < owner_counts).astype(jnp.float32)
    state_old = old_state.reshape(grid_shape) * live[:, :, None, None]
    left_old, right_old = sideways(state_old)
    following = jnp.concatenate([state_old[1:], jnp.zeros_like(state_old[:1])], 0)
    down_old = jnp.take_along_axis(following, downstream[:, :, None, None], axis=1)
    fixed_fwd = source - couple(down_old, face_lift[1], flux_jacobian[:, :, 1]) - couple(left_old, face_lift[2], flux_jacobian[:, :, 2]) - couple(right_old, face_lift[3], flux_jacobian[:, :, 3])

    def forward_step(previous, items):
        fixed_row, inverse_row, jacobian_row, up_row, live_row = items
        nearest = previous[up_row]
        solved = solve_blocks(inverse_row, fixed_row - couple(nearest, face_lift[0], jacobian_row[:, 0]), live_row)
        return solved, solved

    _, half_state = lax.scan(forward_step, jnp.zeros_like(source[0]), (fixed_fwd, block_inverse, flux_jacobian, upstream, live))
    left_half, right_half = sideways(half_state)
    earlier = jnp.concatenate([jnp.zeros_like(half_state[:1]), half_state[:-1]], 0)
    up_new = jnp.take_along_axis(earlier, upstream[:, :, None, None], axis=1)
    fixed_bwd = source - couple(up_new, face_lift[0], flux_jacobian[:, :, 0]) - couple(left_half, face_lift[2], flux_jacobian[:, :, 2]) - couple(right_half, face_lift[3], flux_jacobian[:, :, 3])

    def backward_step(later, items):
        fixed_row, inverse_row, jacobian_row, down_row, live_row = items
        nearest = later[down_row]
        solved = solve_blocks(inverse_row, fixed_row - couple(nearest, face_lift[1], jacobian_row[:, 1]), live_row)
        return solved, solved

    _, full_state = lax.scan(backward_step, jnp.zeros_like(source[0]), (fixed_bwd, block_inverse, flux_jacobian, downstream, live), reverse=True)
    return half_state.reshape(right_side.shape), full_state.reshape(right_side.shape)
```

```python
import functools

import jax
import jax.numpy as jnp
from jax import lax
from jax.experimental import pallas as pl
from jax.experimental.pallas import tpu as pltpu
from jax.sharding import PartitionSpec as P

GROUPS = 4
NVAR = 5
NB = 64
WIDE = 384
STEP_VMEM = 4 << 20
PREP_VMEM = 12 << 20

VMEM_SPEC = pl.BlockSpec(memory_space=pltpu.VMEM)
SMEM_SPEC = pl.BlockSpec(memory_space=pltpu.SMEM)


def dot(a, b):
    return jnp.dot(a, b, preferred_element_type=jnp.float32)


def split(x):
    high = x.astype(jnp.bfloat16)
    low = (x - high.astype(jnp.float32)).astype(jnp.bfloat16)
    return high, low


def couple(x, lift_high, lift_low, mix):
    m = x.shape[0]
    stacked = jnp.concatenate([x[:, :128], x[:, 128:256], x[:, 256:]], axis=0)
    high, low = split(stacked)
    spread = dot(jnp.concatenate([high, low], axis=1), lift_high) + dot(high, lift_low)
    parts = [spread[v // 2 * m : v // 2 * m + m, v % 2 * 128 : v % 2 * 128 + 128] for v in range(NVAR)]
    chunks = []
    for k in range(3):
        at = slice(128 * k, 128 * k + 128)
        total = mix[0][:, at] * parts[0]
        for v in range(1, NVAR):
            total = total + mix[v][:, at] * parts[v]
        chunks.append(total)
    return jnp.concatenate(chunks, axis=1)


def padded(x):
    return jnp.concatenate([x, jnp.zeros((x.shape[0], WIDE - x.shape[1]), x.dtype)], axis=1)


def setup_kernel(
    down_ref, rhs_ref, old_ref, next_ref, left_ref, right_ref, flux_ref, lift_ref,
    fixed_ref, source_ref, mix_ref, high_ref, low_ref, shift_ref, gather_ref,
):
    elems = rhs_ref.shape[0]
    lane = lax.broadcasted_iota(jnp.int32, (elems, 128), 1)
    for d in range(4):
        lift_t = lift_ref[d].T
        both = jnp.concatenate([lift_t, lift_t], axis=1)
        none = jnp.zeros_like(both)
        weight = jnp.concatenate(
            [jnp.concatenate([both, none], axis=1), jnp.concatenate([none, both], axis=1)], axis=0
        )
        high, low = split(weight)
        high_ref[d] = jnp.concatenate([high, high], axis=0)
        low_ref[d] = low
        flux = flux_ref[d]
        for v in range(NVAR):
            for k in range(3):
                u = 2 * k
                first = jnp.broadcast_to(flux[:, 5 * u + v : 5 * u + v + 1], (elems, 128))
                if u + 1 < NVAR:
                    at = 5 * (u + 1) + v
                    second = jnp.broadcast_to(flux[:, at : at + 1], (elems, 128))
                else:
                    second = jnp.zeros((elems, 128), jnp.float32)
                mix_ref[d, v, :, 128 * k : 128 * k + 128] = jnp.where(lane < NB, first, second)
    shift_ref[0:8, :] = jnp.zeros((8, WIDE), jnp.float32)
    shift_ref[elems + 8 : elems + 16, :] = jnp.zeros((8, WIDE), jnp.float32)
    shift_ref[8 : elems + 8, :] = padded(old_ref[...])
    shift_ref[7:8, :] = padded(left_ref[...])
    shift_ref[elems + 8 : elems + 9, :] = padded(right_ref[...])
    gather_ref[...] = jnp.zeros_like(gather_ref)
    for e in range(elems):
        gather_ref[e : e + 1, 0:320] = next_ref[pl.ds(down_ref[0, e], 1), :]
    source = padded(rhs_ref[...])
    source_ref[...] = source

    def face(x, d):
        return couple(x, high_ref[d], low_ref[d], [mix_ref[d, v] for v in range(NVAR)])

    fixed = source - face(gather_ref[...], 1)
    fixed = fixed - face(shift_ref[7 : elems + 7, :], 2)
    fixed_ref[...] = fixed - face(shift_ref[9 : elems + 9, :], 3)


def collect(width, place_ref, parts, out_ref, offset):
    for s, part_ref in enumerate(parts):
        position = s - place_ref[0]

        @pl.when((position >= 0) & (position < GROUPS))
        def _():
            rows = pl.ds(pl.multiple_of(position * width, width) + offset, width)
            out_ref[rows, :] = part_ref[...][:, : out_ref.shape[1]]


def collect_kernel(steps, width, place_ref, *refs):
    collect(width, place_ref, refs[:steps], refs[steps], 0)


def turn_kernel(
    steps, width, place_ref, source_ref, left_ref, right_ref, mix_ref, high_ref, low_ref, *refs
):
    halves, uppers, (fixed_ref, shift_ref, upper_ref) = refs[:steps], refs[steps:2 * steps], refs[2 * steps:]
    elems = source_ref.shape[0]
    shift_ref[0:8, :] = jnp.zeros((8, WIDE), jnp.float32)
    shift_ref[elems + 8 : elems + 16, :] = jnp.zeros((8, WIDE), jnp.float32)
    collect(width, place_ref, halves, shift_ref, 8)
    collect(width, place_ref, uppers, upper_ref, 0)
    shift_ref[7:8, :] = padded(left_ref[...])
    shift_ref[elems + 8 : elems + 9, :] = padded(right_ref[...])

    def face(x, d):
        return couple(x, high_ref[d], low_ref[d], [mix_ref[d, v] for v in range(NVAR)])

    fixed = source_ref[...] - upper_ref[...]
    fixed = fixed - face(shift_ref[7 : elems + 7, :], 2)
    fixed_ref[...] = fixed - face(shift_ref[9 : elems + 9, :], 3)


def step_kernel(
    first_step, sign, face, width, groups,
    place_ref, order_ref, count_ref, message_ref, inverse_ref, fixed_ref, mix_ref, high_ref, low_ref,
    out_ref, state_ref, upper_ref,
):
    position = first_step - sign * place_ref[0]

    @pl.when((position >= 0) & (position < groups))
    def _():
        base = pl.multiple_of(position * width, width)
        rows = pl.ds(base, width)
        mix = [mix_ref[face, v, rows, :] for v in range(NVAR)]
        inflow = couple(message_ref[...], high_ref[face], low_ref[face], mix)
        upper_ref[...] = inflow
        resid = (fixed_ref[rows, :] - inflow)[:, :320].astype(jnp.bfloat16)
        row = lax.broadcasted_iota(jnp.int32, (width, 320), 0)
        solved = jnp.zeros((width, 320), jnp.float32)
        for e in range(width):
            product = lax.dot_general(
                resid, inverse_ref[base + e], (((1,), (1,)), ((), ())),
                preferred_element_type=jnp.float32,
            )
            solved = jnp.where(row == e, product, solved)
        solved = jnp.where(row + base < count_ref[0, 0], solved, 0.0)
        wide = padded(solved)
        state_ref[...] = wide
        for e in range(width):
            out_ref[pl.ds(order_ref[0, base + e] - base, 1), :] = wide[e : e + 1, :]


def step_call(first_step, sign, face, width, groups):
    body = functools.partial(step_kernel, first_step, sign, face, width, groups)
    return pl.pallas_call(
        body,
        out_shape=(jax.ShapeDtypeStruct((width, WIDE), jnp.float32),) * 3,
        in_specs=[SMEM_SPEC] * 3 + [VMEM_SPEC] * 6,
        out_specs=(VMEM_SPEC,) * 3,
        compiler_params=pltpu.CompilerParams(vmem_limit_bytes=STEP_VMEM),
        name="sweep_step",
    )


def edge_rows(cells):
    count = lax.axis_size("cross")
    right = [(i, i + 1) for i in range(count - 1)]
    left = [(i + 1, i) for i in range(count - 1)]
    return lax.ppermute(cells[-1:], "cross", right), lax.ppermute(cells[:1], "cross", left)


def sweep(order, count, place, fixed, inverse, mix, high, low, face, sign, layers):
    elems = fixed.shape[0]
    width = elems // GROUPS
    message = jnp.zeros((width, WIDE), jnp.float32)
    states, uppers = [], []
    for s in range(layers + GROUPS - 1):
        first = s if sign > 0 else s - (layers - 1)
        call = step_call(first, sign, face, width, GROUPS)
        out, state, upper = call(place, order, count, message, inverse, fixed, mix, high, low)
        states.append(state)
        uppers.append(upper)
        turn = [l for l in range(layers - 1) if 0 <= s - l < GROUPS]
        if sign > 0:
            route = [(l, l + 1) for l in turn]
        else:
            route = [(layers - 1 - l, layers - 2 - l) for l in turn]
        if route:
            message = lax.ppermute(out, "flow", route)
    return states, uppers


def collected(place, states, elems):
    steps = len(states)
    body = functools.partial(collect_kernel, steps, elems // GROUPS)
    return pl.pallas_call(
        body,
        out_shape=jax.ShapeDtypeStruct((elems, 320), jnp.float32),
        in_specs=[SMEM_SPEC] + [VMEM_SPEC] * steps,
        out_specs=VMEM_SPEC,
        compiler_params=pltpu.CompilerParams(vmem_limit_bytes=STEP_VMEM),
        name="sweep_collect",
    )(place, *states)


def per_device(
    right_side, old_state, block_inverse, flux_jacobian, face_lift, upstream, downstream, live_counts
):
    layers = lax.axis_size("flow")
    rhs = right_side[0]
    elems = rhs.shape[0]
    inverse = block_inverse[0]
    up = upstream % elems
    down = downstream % elems
    place = lax.axis_index("flow").reshape(1).astype(jnp.int32)
    slot = jnp.arange(elems, dtype=jnp.int32)
    old = jnp.where((slot < live_counts[0, 0])[:, None], old_state[0], 0.0)
    following = lax.ppermute(old, "flow", [(l + 1, l) for l in range(layers - 1)])
    left, right = edge_rows(old)
    flux = jnp.transpose(flux_jacobian[0], (1, 0, 2))
    f32 = jnp.float32
    shift = pltpu.VMEM((elems + 16, WIDE), f32)
    fixed, source, mix, high, low = pl.pallas_call(
        setup_kernel,
        out_shape=(
            jax.ShapeDtypeStruct((elems, WIDE), f32),
            jax.ShapeDtypeStruct((elems, WIDE), f32),
            jax.ShapeDtypeStruct((4, NVAR, elems, WIDE), f32),
            jax.ShapeDtypeStruct((4, 256, 256), jnp.bfloat16),
            jax.ShapeDtypeStruct((4, 128, 256), jnp.bfloat16),
        ),
        in_specs=[SMEM_SPEC] + [VMEM_SPEC] * 7,
        out_specs=(VMEM_SPEC,) * 5,
        scratch_shapes=[shift, pltpu.VMEM((elems, WIDE), f32)],
        compiler_params=pltpu.CompilerParams(vmem_limit_bytes=PREP_VMEM),
        name="sweep_setup",
    )(down, rhs, old, following, left, right, flux, face_lift)
    halves, uppers = sweep(
        down, live_counts, place, fixed, inverse, mix, high, low, 0, 1, layers
    )
    half = collected(place, halves, elems)
    left, right = edge_rows(half)
    steps = len(halves)
    fixed_bwd = pl.pallas_call(
        functools.partial(turn_kernel, steps, elems // GROUPS),
        out_shape=jax.ShapeDtypeStruct((elems, WIDE), f32),
        in_specs=[SMEM_SPEC] + [VMEM_SPEC] * (6 + 2 * steps),
        out_specs=VMEM_SPEC,
        scratch_shapes=[shift, pltpu.VMEM((elems, WIDE), f32)],
        compiler_params=pltpu.CompilerParams(vmem_limit_bytes=PREP_VMEM),
        name="sweep_turn",
    )(place, source, left, right, mix, high, low, *halves, *uppers)
    fulls, _ = sweep(
        up, live_counts, place, fixed_bwd, inverse, mix, high, low, 1, -1, layers
    )
    full = collected(layers - 1 - place, fulls, elems)
    return half[None], full[None]


def solution(mesh):
    in_specs = (
        P("flow", "cross", None),
        P("flow", "cross", None),
        P("flow", "cross", None, None),
        P("flow", "cross", None, None),
        P(),
        P("flow", "cross"),
        P("flow", "cross"),
        P("flow", "cross"),
    )
    out_specs = (P("flow", "cross", None), P("flow", "cross", None))
    return jax.shard_map(
        per_device, mesh=mesh, in_specs=in_specs, out_specs=out_specs, check_vma=False
    )
```

```python
import functools

import jax
import jax.numpy as jnp
from jax import lax
from jax.experimental import pallas as pl
from jax.experimental.pallas import tpu as pltpu
from jax.sharding import PartitionSpec as P

GROUPS = 2
BLOCK = 8
NVAR = 5
NB = 64
WIDE = 384
ORDER = (0, 1)
STEP_VMEM = 3 << 20
PREP_VMEM = 24 << 20

VMEM_SPEC = pl.BlockSpec(memory_space=pltpu.VMEM)
ANY_SPEC = pl.BlockSpec(memory_space=pl.ANY)
F32 = jnp.float32
BF16 = jnp.bfloat16


def dot(a, b):
    return jnp.dot(a, b, preferred_element_type=jnp.float32)


def split(x):
    high = x.astype(jnp.bfloat16)
    low = (x - high.astype(jnp.float32)).astype(jnp.bfloat16)
    return high, low


def couple(x, lift_high, lift_low, mix):
    m = x.shape[0]
    stacked = jnp.concatenate([x[:, :128], x[:, 128:256], x[:, 256:]], axis=0)
    high, low = split(stacked)
    spread = dot(jnp.concatenate([high, low], axis=1), lift_high) + dot(high, lift_low)
    parts = [spread[v // 2 * m : v // 2 * m + m, v % 2 * 128 : v % 2 * 128 + 128] for v in range(NVAR)]
    chunks = []
    for k in range(3):
        at = slice(128 * k, 128 * k + 128)
        total = mix[0][:, at] * parts[0]
        for v in range(1, NVAR):
            total = total + mix[v][:, at] * parts[v]
        chunks.append(total)
    return jnp.concatenate(chunks, axis=1)


def padded(x):
    return jnp.concatenate([x, jnp.zeros((x.shape[0], WIDE - x.shape[1]), x.dtype)], axis=1)


def dot_t(a, b):
    return lax.dot_general(a, b, (((1,), (1,)), ((), ())), preferred_element_type=F32)


def gathered(x, delta):
    rows = x.shape[0]
    cells = x.reshape(rows // 8, 8, x.shape[1])
    chunks = []
    for k in range(3):
        chunk = cells[:, :, 128 * k : 128 * k + 128]
        moved = chunk
        for d in (-3, -2, -1, 1, 2, 3):
            moved = jnp.where(delta.reshape(rows // 8, 8, 128) == d, pltpu.roll(chunk, (-d) % 8, 1), moved)
        chunks.append(moved.reshape(rows, 128))
    return jnp.concatenate(chunks, axis=1)


def load_kernel(
    inverse_ref, flux_ref, lift_ref,
    main_ref, rem_ref, mix_ref, high_ref, low_ref, tail_ref, main_sem, tail_sem,
):
    elems = tail_ref.shape[0]
    tail_copy = pltpu.make_async_copy(inverse_ref.at[:, :, pl.ds(256, 64)], tail_ref, tail_sem)
    main_copy = pltpu.make_async_copy(inverse_ref.at[:, :, pl.ds(0, 256)], main_ref, main_sem)
    tail_copy.start()
    main_copy.start()
    lane = lax.broadcasted_iota(jnp.int32, (elems, 128), 1)
    for d in range(4):
        lift_t = lift_ref[d].T
        both = jnp.concatenate([lift_t, lift_t], axis=1)
        none = jnp.zeros_like(both)
        weight = jnp.concatenate(
            [jnp.concatenate([both, none], axis=1), jnp.concatenate([none, both], axis=1)], axis=0
        )
        high, low = split(weight)
        high_ref[d] = jnp.concatenate([high, high], axis=0)
        low_ref[d] = low
        flux = flux_ref[d]
        for v in range(NVAR):
            for k in range(3):
                u = 2 * k
                first = jnp.broadcast_to(flux[:, 5 * u + v : 5 * u + v + 1], (elems, 128))
                if u + 1 < NVAR:
                    at = 5 * (u + 1) + v
                    second = jnp.broadcast_to(flux[:, at : at + 1], (elems, 128))
                else:
                    second = jnp.zeros((elems, 128), F32)
                mix_ref[d, v, :, 128 * k : 128 * k + 128] = jnp.where(lane < NB, first, second)
    tail_copy.wait()

    @pl.loop(0, elems // 4)
    def _(q):
        rem_ref[q] = jnp.concatenate([tail_ref[4 * q + j] for j in range(4)], axis=1)

    main_copy.wait()


def face_of(x, d, mix_ref, high_ref, low_ref):
    return couple(x, high_ref[d], low_ref[d], [mix_ref[d, v] for v in range(NVAR)])


def beside(shift_ref, left_ref, right_ref):
    elems = shift_ref.shape[0] - 16
    shift_ref[7:8, :] = left_ref[...]
    shift_ref[elems + 8 : elems + 9, :] = right_ref[...]
    return shift_ref[7 : elems + 7, :], shift_ref[9 : elems + 9, :]


def put_groups(fixed, refs):
    width = refs[0].shape[0]
    for p, ref in enumerate(refs):
        ref[...] = fixed[p * width : p * width + width]


def setup_kernel(
    rhs_ref, old_ref, next_ref, left_ref, right_ref, delta_ref, mix_ref, high_ref, low_ref, *refs
):
    fixed_refs, (source_ref, shift_ref) = refs[:GROUPS], refs[GROUPS:]
    elems = rhs_ref.shape[0]
    source = padded(rhs_ref[...])
    source_ref[...] = source
    shift_ref[8 : elems + 8, :] = padded(old_ref[...])
    before, after = beside(shift_ref, left_ref, right_ref)
    below = gathered(padded(next_ref[...]), delta_ref[...])
    fixed = source - face_of(below, 1, mix_ref, high_ref, low_ref)
    fixed = fixed - face_of(before, 2, mix_ref, high_ref, low_ref)
    put_groups(fixed - face_of(after, 3, mix_ref, high_ref, low_ref), fixed_refs)


def turn_kernel(source_ref, left_ref, right_ref, mix_ref, high_ref, low_ref, *refs):
    states, uppers = refs[:GROUPS], refs[GROUPS : 2 * GROUPS]
    fixed_refs, (half_ref, shift_ref) = refs[2 * GROUPS : 3 * GROUPS], refs[3 * GROUPS :]
    width = states[0].shape[0]
    for p in range(GROUPS):
        shift_ref[8 + p * width : 8 + p * width + width, :] = states[p][...]
        half_ref[p * width : p * width + width, :] = states[p][:, :320]
    before, after = beside(shift_ref, left_ref, right_ref)
    fixed = source_ref[...] - jnp.concatenate([upper[...] for upper in uppers], axis=0)
    fixed = fixed - face_of(before, 2, mix_ref, high_ref, low_ref)
    put_groups(fixed - face_of(after, 3, mix_ref, high_ref, low_ref), fixed_refs)


def join_kernel(*refs):
    width = refs[0].shape[0]
    for p in range(GROUPS):
        refs[GROUPS][p * width : p * width + width, :] = refs[p][:, :320]


def step_kernel(
    layer, face, group, keep,
    message_ref, main_ref, rem_ref, fixed_ref, mix_ref, high_ref, low_ref, delta_ref, live_ref,
    token_ref, *refs,
):
    del token_ref
    count = 2 if keep else 1
    held_refs, (out_ref, *new_refs, body_ref) = refs[:count], refs[count:]
    width = message_ref.shape[0]
    active = lax.axis_index("flow") == layer

    @pl.when(active)
    def _():
        base = group * width
        rows = pl.ds(base, width)
        mix = [mix_ref[face, v, rows, :] for v in range(NVAR)]
        inflow = couple(gathered(message_ref[...], delta_ref[rows, :]), high_ref[face], low_ref[face], mix)
        if keep:
            new_refs[1][...] = inflow
        resid = fixed_ref[...] - inflow
        tail = resid[:, 256:]
        tail = tail + pltpu.roll(tail, 64, 1)
        row = lax.broadcasted_iota(jnp.int32, (width, 256), 0)
        lane = lax.broadcasted_iota(jnp.int32, (width, 256), 1)
        body_ref[:, :256] = resid[:, :256]
        body_ref[:, 256:] = jnp.where(row % 4 == lane // 64, jnp.concatenate([tail, tail], axis=1), 0.0)
        at = lax.broadcasted_iota(jnp.int32, (BLOCK, 320), 0)

        @pl.loop(0, width // BLOCK)
        def _(b):
            part = pl.ds(pl.multiple_of(b * BLOCK, BLOCK), BLOCK)
            both = body_ref[part, :].astype(BF16)
            first = base + b * BLOCK
            rest = jnp.zeros((BLOCK, 320), F32)
            solved = jnp.zeros((BLOCK, 320), F32)
            for q in range(BLOCK // 4):
                rest = jnp.where(at // 4 == q, dot_t(both[:, 256:], rem_ref[first // 4 + q]), rest)
                for e in range(4 * q, 4 * q + 4):
                    solved = jnp.where(at == e, dot_t(both[:, :256], main_ref[first + e]), solved)
            wide = padded(solved + rest)
            live = live_ref[pl.ds(pl.multiple_of(first, BLOCK), BLOCK), :]
            wide = wide * jnp.concatenate([live, live, live], axis=1)
            new_refs[0][part, :] = wide
            out_ref[part, :] = wide

    @pl.when(jnp.logical_not(active))
    def _():
        for held, new in zip(held_refs, new_refs):
            new[...] = held[...]


def step_call(layer, face, group, keep, width):
    body = functools.partial(step_kernel, layer, face, group, keep)
    count = 2 if keep else 1
    cells = jax.ShapeDtypeStruct((width, WIDE), F32)
    return pl.pallas_call(
        body,
        out_shape=(cells,) * (1 + count),
        in_specs=[VMEM_SPEC] * 9 + [ANY_SPEC] + [VMEM_SPEC] * count,
        out_specs=(VMEM_SPEC,) * (1 + count),
        scratch_shapes=[pltpu.VMEM((width, 512), F32)],
        compiler_params=pltpu.CompilerParams(vmem_limit_bytes=STEP_VMEM),
        cost_estimate=pl.CostEstimate(flops=width * 320 * 320 * 2, bytes_accessed=width * 320 * 320 * 2, transcendentals=0),
        name="sweep_step",
    )


def edge_rows(first, last):
    count = lax.axis_size("cross")
    right = [(i, i + 1) for i in range(count - 1)]
    left = [(i + 1, i) for i in range(count - 1)]
    return lax.ppermute(last, "cross", right), lax.ppermute(first, "cross", left)


def sweep(fixed, table, delta, live, face, keep, route):
    width = fixed[0].shape[0]
    blank = jnp.zeros((width, WIDE), F32)
    messages = [blank] * GROUPS
    held = [(blank,) * (2 if keep else 1)] * GROUPS
    token = fixed[0]
    last = len(route) - 1
    for i, layer in enumerate(route):
        for p in ORDER:
            call = step_call(layer, face, p, keep, width)
            main, rem, mix, high, low = table
            out, *new = call(
                messages[p], main, rem, fixed[p], mix, high, low, delta, live, token, *held[p]
            )
            token = out
            held[p] = tuple(new)
            if i < last:
                messages[p] = lax.ppermute(out, "flow", [(i, i + 1), (last - i, last - i - 1)])
    return held


def per_device(
    right_side, old_state, block_inverse, flux_jacobian, face_lift, upstream, downstream, live_counts
):
    layers = lax.axis_size("flow")
    rhs = right_side[0]
    elems = rhs.shape[0]
    width = elems // GROUPS
    slot = jnp.arange(elems, dtype=jnp.int32)[:, None]
    up = jnp.broadcast_to(upstream[0][:, None] % elems - slot, (elems, 128))
    down = jnp.broadcast_to(downstream[0][:, None] % elems - slot, (elems, 128))
    live = jnp.broadcast_to((slot < live_counts[0, 0]).astype(F32), (elems, 128))
    old = jnp.where(slot < live_counts[0, 0], old_state[0], 0.0)
    following = lax.ppermute(old, "flow", [(l + 1, l) for l in range(layers - 1)])
    edge = jnp.pad(old[:1], ((0, 0), (0, WIDE - 320))), jnp.pad(old[-1:], ((0, 0), (0, WIDE - 320)))
    left, right = edge_rows(*edge)
    flux = jnp.transpose(flux_jacobian[0], (1, 0, 2))
    shift = pltpu.VMEM((elems + 16, WIDE), F32)
    cells = jax.ShapeDtypeStruct((elems, WIDE), F32)
    group_cells = (jax.ShapeDtypeStruct((width, WIDE), F32),) * GROUPS
    prep = pltpu.CompilerParams(vmem_limit_bytes=PREP_VMEM)
    table = pl.pallas_call(
        load_kernel,
        out_shape=(
            jax.ShapeDtypeStruct((elems, 320, 256), BF16),
            jax.ShapeDtypeStruct((elems // 4, 320, 256), BF16),
            jax.ShapeDtypeStruct((4, NVAR, elems, WIDE), F32),
            jax.ShapeDtypeStruct((4, 256, 256), BF16),
            jax.ShapeDtypeStruct((4, 128, 256), BF16),
        ),
        in_specs=[ANY_SPEC] + [VMEM_SPEC] * 2,
        out_specs=(VMEM_SPEC,) * 5,
        scratch_shapes=[
            pltpu.VMEM((elems, 320, 64), BF16), pltpu.SemaphoreType.DMA, pltpu.SemaphoreType.DMA
        ],
        compiler_params=prep,
        name="sweep_load",
    )(block_inverse[0], flux, face_lift)
    mixing = table[2:]
    *fixed, source = pl.pallas_call(
        setup_kernel,
        out_shape=group_cells + (cells,),
        in_specs=[VMEM_SPEC] * 9,
        out_specs=(VMEM_SPEC,) * (GROUPS + 1),
        scratch_shapes=[shift],
        compiler_params=prep,
        name="sweep_setup",
    )(rhs, old, following, left, right, down, *mixing)
    held = sweep(fixed, table, up, live, 0, True, list(range(layers)))
    states = [state for state, _ in held]
    uppers = [upper for _, upper in held]
    left, right = edge_rows(states[0][:1], states[-1][-1:])
    *fixed, half = pl.pallas_call(
        turn_kernel,
        out_shape=group_cells + (jax.ShapeDtypeStruct((elems, 320), F32),),
        in_specs=[VMEM_SPEC] * (6 + 2 * GROUPS),
        out_specs=(VMEM_SPEC,) * (GROUPS + 1),
        scratch_shapes=[shift],
        compiler_params=prep,
        name="sweep_turn",
    )(source, left, right, *mixing, *states, *uppers)
    held = sweep(fixed, table, down, live, 1, False, list(reversed(range(layers))))
    full = pl.pallas_call(
        join_kernel,
        out_shape=jax.ShapeDtypeStruct((elems, 320), F32),
        in_specs=[VMEM_SPEC] * GROUPS,
        out_specs=VMEM_SPEC,
        compiler_params=pltpu.CompilerParams(vmem_limit_bytes=STEP_VMEM),
        name="sweep_join",
    )(*[state for state, in held])
    return half[None], full[None]


def solution(mesh):
    in_specs = (
        P("flow", "cross", None),
        P("flow", "cross", None),
        P("flow", "cross", None, None),
        P("flow", "cross", None, None),
        P(),
        P("flow", "cross"),
        P("flow", "cross"),
        P("flow", "cross"),
    )
    out_specs = (P("flow", "cross", None), P("flow", "cross", None))
    return jax.shard_map(
        per_device, mesh=mesh, in_specs=in_specs, out_specs=out_specs, check_vma=False
    )
```

```python
import functools

import jax
import jax.numpy as jnp
from jax import lax
from jax.experimental import pallas as pl
from jax.experimental.pallas import tpu as pltpu
from jax.sharding import PartitionSpec as P

GROUPS = 4
BLOCK = 8
NVAR = 5
NB = 64
WIDE = 384
ORDER = (0, 3, 1, 2)
SPAN = 4
STEP_VMEM = 3 << 20
PREP_VMEM = 24 << 20

VMEM_SPEC = pl.BlockSpec(memory_space=pltpu.VMEM)
ANY_SPEC = pl.BlockSpec(memory_space=pl.ANY)
F32 = jnp.float32
BF16 = jnp.bfloat16


def dot(a, b):
    return jnp.dot(a, b, preferred_element_type=jnp.float32)


def split(x):
    high = x.astype(jnp.bfloat16)
    low = (x - high.astype(jnp.float32)).astype(jnp.bfloat16)
    return high, low


def couple(x, lift_high, lift_low, mix):
    m = x.shape[0]
    stacked = jnp.concatenate([x[:, :128], x[:, 128:256], x[:, 256:]], axis=0)
    high, low = split(stacked)
    spread = dot(jnp.concatenate([high, low], axis=1), lift_high) + dot(high, lift_low)
    parts = [spread[v // 2 * m : v // 2 * m + m, v % 2 * 128 : v % 2 * 128 + 128] for v in range(NVAR)]
    chunks = []
    for k in range(3):
        at = slice(128 * k, 128 * k + 128)
        total = mix[0][:, at] * parts[0]
        for v in range(1, NVAR):
            total = total + mix[v][:, at] * parts[v]
        chunks.append(total)
    return jnp.concatenate(chunks, axis=1)


def padded(x):
    return jnp.concatenate([x, jnp.zeros((x.shape[0], WIDE - x.shape[1]), x.dtype)], axis=1)


def dot_t(a, b):
    return lax.dot_general(a, b, (((1,), (1,)), ((), ())), preferred_element_type=F32)


def gathered(x, delta):
    rows = x.shape[0]
    cells = x.reshape(rows // 8, 8, x.shape[1])
    chunks = []
    for k in range(3):
        chunk = cells[:, :, 128 * k : 128 * k + 128]
        moved = chunk
        for d in (-3, -2, -1, 1, 2, 3):
            moved = jnp.where(delta.reshape(rows // 8, 8, 128) == d, pltpu.roll(chunk, (-d) % 8, 1), moved)
        chunks.append(moved.reshape(rows, 128))
    return jnp.concatenate(chunks, axis=1)


def load_kernel(
    inverse_ref, flux_ref, lift_ref,
    main_ref, rem_ref, mix_ref, high_ref, low_ref, tail_ref, main_sem, tail_sem,
):
    elems = tail_ref.shape[0]
    tail_copy = pltpu.make_async_copy(inverse_ref.at[:, :, pl.ds(256, 64)], tail_ref, tail_sem)
    main_copy = pltpu.make_async_copy(inverse_ref.at[:, :, pl.ds(0, 256)], main_ref, main_sem)
    tail_copy.start()
    main_copy.start()
    lane = lax.broadcasted_iota(jnp.int32, (elems, 128), 1)
    for d in range(4):
        lift_t = lift_ref[d].T
        both = jnp.concatenate([lift_t, lift_t], axis=1)
        none = jnp.zeros_like(both)
        weight = jnp.concatenate(
            [jnp.concatenate([both, none], axis=1), jnp.concatenate([none, both], axis=1)], axis=0
        )
        high, low = split(weight)
        high_ref[d] = jnp.concatenate([high, high], axis=0)
        low_ref[d] = low
        flux = flux_ref[d]
        for v in range(NVAR):
            for k in range(3):
                u = 2 * k
                first = jnp.broadcast_to(flux[:, 5 * u + v : 5 * u + v + 1], (elems, 128))
                if u + 1 < NVAR:
                    at = 5 * (u + 1) + v
                    second = jnp.broadcast_to(flux[:, at : at + 1], (elems, 128))
                else:
                    second = jnp.zeros((elems, 128), F32)
                mix_ref[d, v, :, 128 * k : 128 * k + 128] = jnp.where(lane < NB, first, second)
    tail_copy.wait()

    @pl.loop(0, elems // 4)
    def _(q):
        rem_ref[q] = jnp.concatenate([tail_ref[4 * q + j] for j in range(4)], axis=1)

    main_copy.wait()


def face_of(x, d, mix_ref, high_ref, low_ref):
    return couple(x, high_ref[d], low_ref[d], [mix_ref[d, v] for v in range(NVAR)])


def beside(shift_ref, left_ref, right_ref):
    elems = shift_ref.shape[0] - 16
    shift_ref[7:8, :] = left_ref[...]
    shift_ref[elems + 8 : elems + 9, :] = right_ref[...]
    return shift_ref[7 : elems + 7, :], shift_ref[9 : elems + 9, :]


def put_groups(fixed, refs):
    width = refs[0].shape[0]
    for p, ref in enumerate(refs):
        ref[...] = fixed[p * width : p * width + width]


def setup_kernel(
    rhs_ref, old_ref, next_ref, left_ref, right_ref, delta_ref, mix_ref, high_ref, low_ref, *refs
):
    fixed_refs, (source_ref, shift_ref) = refs[:GROUPS], refs[GROUPS:]
    elems = rhs_ref.shape[0]
    source = padded(rhs_ref[...])
    source_ref[...] = source
    shift_ref[8 : elems + 8, :] = padded(old_ref[...])
    before, after = beside(shift_ref, left_ref, right_ref)
    below = gathered(padded(next_ref[...]), delta_ref[...])
    fixed = source - face_of(below, 1, mix_ref, high_ref, low_ref)
    fixed = fixed - face_of(before, 2, mix_ref, high_ref, low_ref)
    put_groups(fixed - face_of(after, 3, mix_ref, high_ref, low_ref), fixed_refs)


def turn_kernel(source_ref, left_ref, right_ref, mix_ref, high_ref, low_ref, *refs):
    states, uppers = refs[:GROUPS], refs[GROUPS : 2 * GROUPS]
    fixed_refs, (half_ref, shift_ref) = refs[2 * GROUPS : 3 * GROUPS], refs[3 * GROUPS :]
    width = states[0].shape[0]
    for p in range(GROUPS):
        shift_ref[8 + p * width : 8 + p * width + width, :] = states[p][...]
        half_ref[p * width : p * width + width, :] = states[p][:, :320]
    before, after = beside(shift_ref, left_ref, right_ref)
    fixed = source_ref[...] - jnp.concatenate([upper[...] for upper in uppers], axis=0)
    fixed = fixed - face_of(before, 2, mix_ref, high_ref, low_ref)
    put_groups(fixed - face_of(after, 3, mix_ref, high_ref, low_ref), fixed_refs)


def join_kernel(*refs):
    width = refs[0].shape[0]
    for p in range(GROUPS):
        refs[GROUPS][p * width : p * width + width, :] = refs[p][:, :320]


def step_kernel(
    layer, face, group, keep,
    message_ref, main_ref, rem_ref, fixed_ref, mix_ref, high_ref, low_ref, delta_ref, live_ref,
    token_ref, *refs,
):
    del token_ref
    count = 2 if keep else 1
    held_refs, new_refs, (body_ref,) = refs[:count], refs[count : 2 * count], refs[2 * count :]
    width = message_ref.shape[0]
    active = lax.axis_index("flow") == layer

    @pl.when(active)
    def _():
        base = group * width
        rows = pl.ds(base, width)
        mix = [mix_ref[face, v, rows, :] for v in range(NVAR)]
        inflow = couple(gathered(message_ref[...], delta_ref[rows, :]), high_ref[face], low_ref[face], mix)
        if keep:
            new_refs[1][...] = inflow
        resid = fixed_ref[...] - inflow
        tail = resid[:, 256:]
        tail = tail + pltpu.roll(tail, 64, 1)
        row = lax.broadcasted_iota(jnp.int32, (width, 256), 0)
        lane = lax.broadcasted_iota(jnp.int32, (width, 256), 1)
        body_ref[:, :256] = resid[:, :256]
        body_ref[:, 256:] = jnp.where(row % 4 == lane // 64, jnp.concatenate([tail, tail], axis=1), 0.0)
        at = lax.broadcasted_iota(jnp.int32, (BLOCK, 320), 0)

        @pl.loop(0, width // BLOCK)
        def _(b):
            part = pl.ds(pl.multiple_of(b * BLOCK, BLOCK), BLOCK)
            both = body_ref[part, :].astype(BF16)
            first = base + b * BLOCK
            rest = jnp.zeros((BLOCK, 320), F32)
            solved = jnp.zeros((BLOCK, 320), F32)
            for q in range(BLOCK // 4):
                rest = jnp.where(at // 4 == q, dot_t(both[:, 256:], rem_ref[first // 4 + q]), rest)
                for e in range(4 * q, 4 * q + 4):
                    solved = jnp.where(at == e, dot_t(both[:, :256], main_ref[first + e]), solved)
            wide = padded(solved + rest)
            live = live_ref[pl.ds(pl.multiple_of(first, BLOCK), BLOCK), :]
            wide = wide * jnp.concatenate([live, live, live], axis=1)
            new_refs[0][part, :] = wide

    @pl.when(jnp.logical_not(active))
    def _():
        for held, new in zip(held_refs, new_refs):
            new[...] = held[...]


def step_call(layer, face, group, keep, width):
    body = functools.partial(step_kernel, layer, face, group, keep)
    count = 2 if keep else 1
    cells = jax.ShapeDtypeStruct((width, WIDE), F32)
    return pl.pallas_call(
        body,
        out_shape=(cells,) * count,
        in_specs=[VMEM_SPEC] * 9 + [ANY_SPEC] + [VMEM_SPEC] * count,
        out_specs=(VMEM_SPEC,) * count,
        scratch_shapes=[pltpu.VMEM((width, 512), F32)],
        compiler_params=pltpu.CompilerParams(vmem_limit_bytes=STEP_VMEM),
        cost_estimate=pl.CostEstimate(flops=width * 320 * 320 * 2, bytes_accessed=width * 320 * 320 * 2, transcendentals=0),
        name="sweep_step",
    )


def edge_rows(first, last):
    count = lax.axis_size("cross")
    right = [(i, i + 1) for i in range(count - 1)]
    left = [(i + 1, i) for i in range(count - 1)]
    return lax.ppermute(last, "cross", right), lax.ppermute(first, "cross", left)


def sweep(fixed, table, delta, live, face, keep, route):
    width = fixed[0].shape[0]
    blank = jnp.zeros((width, WIDE), F32)
    messages = [blank] * GROUPS
    held = [(blank,) * (2 if keep else 1)] * GROUPS
    token = fixed[0]
    last = len(route) - 1
    for i, layer in enumerate(route):
        for p in ORDER:
            call = step_call(layer, face, p, keep, width)
            main, rem, mix, high, low = table
            new = call(
                messages[p], main, rem, fixed[p], mix, high, low, delta, live, token, *held[p]
            )
            token = new[0]
            held[p] = tuple(new)
            if i < last:
                pairs = [(route[k], route[k + 1]) for k in range(i % SPAN, last, SPAN)]
                messages[p] = lax.ppermute(token, "flow", pairs)
    return held


def per_device(
    right_side, old_state, block_inverse, flux_jacobian, face_lift, upstream, downstream, live_counts
):
    layers = lax.axis_size("flow")
    rhs = right_side[0]
    elems = rhs.shape[0]
    width = elems // GROUPS
    slot = jnp.arange(elems, dtype=jnp.int32)[:, None]
    alive = slot < live_counts[0, 0]
    up = jnp.broadcast_to(upstream[0][:, None] % elems - slot, (elems, 128))
    down = jnp.broadcast_to(downstream[0][:, None] % elems - slot, (elems, 128))
    live = jnp.broadcast_to(alive.astype(F32), (elems, 128))
    old = jnp.where(alive, old_state[0], 0.0)
    following = lax.ppermute(old, "flow", [(l + 1, l) for l in range(layers - 1)])
    edge = jnp.pad(old[:1], ((0, 0), (0, WIDE - 320))), jnp.pad(old[-1:], ((0, 0), (0, WIDE - 320)))
    left, right = edge_rows(*edge)
    flux = jnp.transpose(flux_jacobian[0], (1, 0, 2))
    shift = pltpu.VMEM((elems + 16, WIDE), F32)
    cells = jax.ShapeDtypeStruct((elems, WIDE), F32)
    group_cells = (jax.ShapeDtypeStruct((width, WIDE), F32),) * GROUPS
    prep = pltpu.CompilerParams(vmem_limit_bytes=PREP_VMEM)
    table = pl.pallas_call(
        load_kernel,
        out_shape=(
            jax.ShapeDtypeStruct((elems, 320, 256), BF16),
            jax.ShapeDtypeStruct((elems // 4, 320, 256), BF16),
            jax.ShapeDtypeStruct((4, NVAR, elems, WIDE), F32),
            jax.ShapeDtypeStruct((4, 256, 256), BF16),
            jax.ShapeDtypeStruct((4, 128, 256), BF16),
        ),
        in_specs=[ANY_SPEC] + [VMEM_SPEC] * 2,
        out_specs=(VMEM_SPEC,) * 5,
        scratch_shapes=[
            pltpu.VMEM((elems, 320, 64), BF16), pltpu.SemaphoreType.DMA, pltpu.SemaphoreType.DMA
        ],
        compiler_params=prep,
        name="sweep_load",
    )(block_inverse[0], flux, face_lift)
    mixing = table[2:]
    *fixed, source = pl.pallas_call(
        setup_kernel,
        out_shape=group_cells + (cells,),
        in_specs=[VMEM_SPEC] * 9,
        out_specs=(VMEM_SPEC,) * (GROUPS + 1),
        scratch_shapes=[shift],
        compiler_params=prep,
        name="sweep_setup",
    )(rhs, old, following, left, right, down, *mixing)
    held = sweep(fixed, table, up, live, 0, True, list(range(layers)))
    states = [state for state, _ in held]
    uppers = [upper for _, upper in held]
    left, right = edge_rows(states[0][:1], states[-1][-1:])
    *fixed, half = pl.pallas_call(
        turn_kernel,
        out_shape=group_cells + (jax.ShapeDtypeStruct((elems, 320), F32),),
        in_specs=[VMEM_SPEC] * (6 + 2 * GROUPS),
        out_specs=(VMEM_SPEC,) * (GROUPS + 1),
        scratch_shapes=[shift],
        compiler_params=prep,
        name="sweep_turn",
    )(source, left, right, *mixing, *states, *uppers)
    held = sweep(fixed, table, down, live, 1, False, list(reversed(range(layers))))
    full = pl.pallas_call(
        join_kernel,
        out_shape=jax.ShapeDtypeStruct((elems, 320), F32),
        in_specs=[VMEM_SPEC] * GROUPS,
        out_specs=VMEM_SPEC,
        compiler_params=pltpu.CompilerParams(vmem_limit_bytes=STEP_VMEM),
        name="sweep_join",
    )(*[state for state, in held])
    return half[None], full[None]


def solution(mesh):
    in_specs = (
        P("flow", "cross", None),
        P("flow", "cross", None),
        P("flow", "cross", None, None),
        P("flow", "cross", None, None),
        P(),
        P("flow", "cross"),
        P("flow", "cross"),
        P("flow", "cross"),
    )
    out_specs = (P("flow", "cross", None), P("flow", "cross", None))
    return jax.shard_map(
        per_device, mesh=mesh, in_specs=in_specs, out_specs=out_specs, check_vma=False
    )
```

```python
import functools

import jax
import jax.numpy as jnp
from jax import lax
from jax.experimental import pallas as pl
from jax.experimental.pallas import tpu as pltpu
from jax.sharding import PartitionSpec as P

GROUPS = 4
BLOCK = 8
NVAR = 5
NB = 64
WIDE = 384
ORDER = (0, 3, 1, 2)
SPAN = 4
STEP_VMEM = 3 << 20
PREP_VMEM = 24 << 20

VMEM_SPEC = pl.BlockSpec(memory_space=pltpu.VMEM)
ANY_SPEC = pl.BlockSpec(memory_space=pl.ANY)
F32 = jnp.float32
BF16 = jnp.bfloat16


def dot(a, b):
    return jnp.dot(a, b, preferred_element_type=jnp.float32)


def split(x):
    high = x.astype(jnp.bfloat16)
    low = (x - high.astype(jnp.float32)).astype(jnp.bfloat16)
    return high, low


def couple(x, lift_high, lift_low, mix):
    m = x.shape[0]
    stacked = jnp.concatenate([x[:, :128], x[:, 128:256], x[:, 256:]], axis=0)
    high, low = split(stacked)
    if lift_low is None:
        spread = dot(high, lift_high[:128])
    else:
        spread = dot(jnp.concatenate([high, low], axis=1), lift_high) + dot(high, lift_low)
    parts = [spread[v // 2 * m : v // 2 * m + m, v % 2 * 128 : v % 2 * 128 + 128] for v in range(NVAR)]
    chunks = []
    for k in range(3):
        at = slice(128 * k, 128 * k + 128)
        total = mix[0][:, at] * parts[0]
        for v in range(1, NVAR):
            total = total + mix[v][:, at] * parts[v]
        chunks.append(total)
    return jnp.concatenate(chunks, axis=1)


def padded(x):
    return jnp.concatenate([x, jnp.zeros((x.shape[0], WIDE - x.shape[1]), x.dtype)], axis=1)


def dot_t(a, b):
    return lax.dot_general(a, b, (((1,), (1,)), ((), ())), preferred_element_type=F32)


def gathered(x, delta):
    rows = x.shape[0]
    cells = x.reshape(rows // 8, 8, x.shape[1])
    chunks = []
    for k in range(3):
        chunk = cells[:, :, 128 * k : 128 * k + 128]
        moved = chunk
        for d in (-3, -2, -1, 1, 2, 3):
            moved = jnp.where(delta.reshape(rows // 8, 8, 128) == d, pltpu.roll(chunk, (-d) % 8, 1), moved)
        chunks.append(moved.reshape(rows, 128))
    return jnp.concatenate(chunks, axis=1)


def load_kernel(
    count_ref, inverse_ref, flux_ref, lift_hbm, up_ref, down_ref,
    main_ref, rem_ref, mix_ref, high_ref, low_ref, up_out, down_out, live_ref,
    flux_buf, lift_ref, slots, sems,
):
    elems = main_ref.shape[0]
    width = elems // GROUPS
    small = [
        pltpu.make_async_copy(src, dst, sems.at[GROUPS + n])
        for n, (src, dst) in enumerate(
            [(flux_ref, flux_buf), (lift_hbm, lift_ref), (up_ref, slots.at[0]), (down_ref, slots.at[1])]
        )
    ]
    large = []
    for p in range(GROUPS):
        rows = pl.ds(p * width, width)
        large.append(pltpu.make_async_copy(inverse_ref.at[rows], main_ref.at[rows], sems.at[p]))
    for copy in small + large:
        copy.start()
    for copy in small:
        copy.wait()
    row = lax.broadcasted_iota(jnp.int32, (elems, 128), 0)
    for n, out in enumerate((up_out, down_out)):
        local = (slots[n] & (elems - 1)).astype(F32)
        out[...] = jnp.broadcast_to(local, (128, elems)).T - row.astype(F32)
    live_ref[...] = jnp.where(row < count_ref[0, 0], 1.0, 0.0)
    lane = lax.broadcasted_iota(jnp.int32, (elems, 128), 1)
    for d in range(4):
        lift_t = lift_ref[d].T
        both = jnp.concatenate([lift_t, lift_t], axis=1)
        none = jnp.zeros_like(both)
        weight = jnp.concatenate(
            [jnp.concatenate([both, none], axis=1), jnp.concatenate([none, both], axis=1)], axis=0
        )
        high, low = split(weight)
        high_ref[d] = jnp.concatenate([high, high], axis=0)
        low_ref[d] = low
        flux = flux_buf[:, d, :]
        flux = jnp.concatenate([flux, jnp.zeros((7, elems), F32)], axis=0).T
        for v in range(NVAR):
            for k in range(3):
                u = 2 * k
                first = jnp.broadcast_to(flux[:, 5 * u + v : 5 * u + v + 1], (elems, 128))
                if u + 1 < NVAR:
                    at = 5 * (u + 1) + v
                    second = jnp.broadcast_to(flux[:, at : at + 1], (elems, 128))
                else:
                    second = jnp.zeros((elems, 128), F32)
                mix_ref[d, v, :, 128 * k : 128 * k + 128] = jnp.where(lane < NB, first, second)
    for p in range(GROUPS):
        large[p].wait()

        @pl.loop(p * width // 4, (p + 1) * width // 4)
        def _(q):
            rem_ref[q] = jnp.concatenate([main_ref[4 * q + j, :, 256:320] for j in range(4)], axis=1)


def face_of(x, d, mix_ref, high_ref, low_ref):
    return couple(x, high_ref[d], low_ref[d], [mix_ref[d, v] for v in range(NVAR)])


def beside(shift_ref, left_ref, right_ref):
    elems = shift_ref.shape[0] - 16
    shift_ref[7:8, :] = left_ref[...]
    shift_ref[elems + 8 : elems + 9, :] = right_ref[...]
    return shift_ref[7 : elems + 7, :], shift_ref[9 : elems + 9, :]


def put_groups(fixed, refs):
    width = refs[0].shape[0]
    for p, ref in enumerate(refs):
        ref[...] = fixed[p * width : p * width + width]


def setup_kernel(
    rhs_ref, old_ref, next_ref, left_ref, right_ref, delta_ref, mix_ref, high_ref, low_ref, *refs
):
    fixed_refs, (source_ref, shift_ref) = refs[:GROUPS], refs[GROUPS:]
    elems = rhs_ref.shape[0]
    source = padded(rhs_ref[...])
    source_ref[...] = source
    shift_ref[8 : elems + 8, :] = padded(old_ref[...])
    before, after = beside(shift_ref, left_ref, right_ref)
    below = gathered(padded(next_ref[...]), delta_ref[...])
    fixed = source - face_of(below, 1, mix_ref, high_ref, low_ref)
    fixed = fixed - face_of(before, 2, mix_ref, high_ref, low_ref)
    put_groups(fixed - face_of(after, 3, mix_ref, high_ref, low_ref), fixed_refs)


def turn_kernel(source_ref, left_ref, right_ref, mix_ref, high_ref, low_ref, *refs):
    states, uppers = refs[:GROUPS], refs[GROUPS : 2 * GROUPS]
    fixed_refs, (half_ref, shift_ref) = refs[2 * GROUPS : 3 * GROUPS], refs[3 * GROUPS :]
    width = states[0].shape[0]
    for p in range(GROUPS):
        shift_ref[8 + p * width : 8 + p * width + width, :] = states[p][...]
        half_ref[p * width : p * width + width, :] = states[p][:, :320]
    before, after = beside(shift_ref, left_ref, right_ref)
    fixed = source_ref[...] - jnp.concatenate([upper[...] for upper in uppers], axis=0)
    fixed = fixed - face_of(before, 2, mix_ref, high_ref, low_ref)
    put_groups(fixed - face_of(after, 3, mix_ref, high_ref, low_ref), fixed_refs)


def join_kernel(*refs):
    width = refs[0].shape[0]
    for p in range(GROUPS):
        refs[GROUPS][p * width : p * width + width, :] = refs[p][:, :320]


def step_kernel(
    layer, face, group, keep,
    message_ref, main_ref, rem_ref, fixed_ref, mix_ref, high_ref, delta_ref, live_ref,
    token_ref, *refs,
):
    del token_ref
    count = 2 if keep else 1
    held_refs, new_refs, (body_ref,) = refs[:count], refs[count : 2 * count], refs[2 * count :]
    width = message_ref.shape[0]
    active = lax.axis_index("flow") == layer

    @pl.when(active)
    def _():
        base = group * width
        rows = pl.ds(base, width)
        mix = [mix_ref[face, v, rows, :] for v in range(NVAR)]
        inflow = couple(gathered(message_ref[...], delta_ref[rows, :]), high_ref[face], None, mix)
        if keep:
            new_refs[1][...] = inflow
        resid = fixed_ref[...] - inflow
        tail = resid[:, 256:]
        tail = tail + pltpu.roll(tail, 64, 1)
        row = lax.broadcasted_iota(jnp.int32, (width, 256), 0)
        lane = lax.broadcasted_iota(jnp.int32, (width, 256), 1)
        body_ref[:, :256] = resid[:, :256]
        body_ref[:, 256:] = jnp.where(row % 4 == lane // 64, jnp.concatenate([tail, tail], axis=1), 0.0)
        at = lax.broadcasted_iota(jnp.int32, (BLOCK, 320), 0)

        @pl.loop(0, width // BLOCK)
        def _(b):
            part = pl.ds(pl.multiple_of(b * BLOCK, BLOCK), BLOCK)
            both = body_ref[part, :].astype(BF16)
            first = base + b * BLOCK
            rest = jnp.zeros((BLOCK, 320), F32)
            solved = jnp.zeros((BLOCK, 320), F32)
            for q in range(BLOCK // 4):
                rest = jnp.where(at // 4 == q, dot_t(both[:, 256:], rem_ref[first // 4 + q]), rest)
                for e in range(4 * q, 4 * q + 4):
                    solved = jnp.where(at == e, dot_t(both[:, :256], main_ref[first + e, :, :256]), solved)
            wide = padded(solved + rest)
            live = live_ref[pl.ds(pl.multiple_of(first, BLOCK), BLOCK), :]
            wide = wide * jnp.concatenate([live, live, live], axis=1)
            new_refs[0][part, :] = wide

    @pl.when(jnp.logical_not(active))
    def _():
        for held, new in zip(held_refs, new_refs):
            new[...] = held[...]


def step_call(layer, face, group, keep, width):
    body = functools.partial(step_kernel, layer, face, group, keep)
    count = 2 if keep else 1
    cells = jax.ShapeDtypeStruct((width, WIDE), F32)
    return pl.pallas_call(
        body,
        out_shape=(cells,) * count,
        in_specs=[VMEM_SPEC] * 8 + [ANY_SPEC] + [VMEM_SPEC] * count,
        out_specs=(VMEM_SPEC,) * count,
        scratch_shapes=[pltpu.VMEM((width, 512), F32)],
        compiler_params=pltpu.CompilerParams(
            vmem_limit_bytes=STEP_VMEM
        ),
        cost_estimate=pl.CostEstimate(flops=width * 320 * 320 * 2, bytes_accessed=width * 320 * 320 * 2, transcendentals=0),
        name="sweep_step",
    )


def edge_rows(first, last):
    count = lax.axis_size("cross")
    right = [(i, i + 1) for i in range(count - 1)]
    left = [(i + 1, i) for i in range(count - 1)]
    return lax.ppermute(last, "cross", right), lax.ppermute(first, "cross", left)


def sweep(fixed, table, delta, live, face, keep, route):
    width = fixed[0].shape[0]
    blank = jnp.zeros((width, WIDE), F32)
    messages = [blank] * GROUPS
    held = [(blank,) * (2 if keep else 1)] * GROUPS
    token = fixed[0]
    last = len(route) - 1
    for i, layer in enumerate(route):
        for p in ORDER:
            call = step_call(layer, face, p, keep, width)
            main, rem, mix, high = table[:4]
            new = call(messages[p], main, rem, fixed[p], mix, high, delta, live, token, *held[p])
            token = new[0]
            held[p] = tuple(new)
            if i < last:
                pairs = [(route[k], route[k + 1]) for k in range(i % SPAN, last, SPAN)]
                messages[p] = lax.ppermute(token, "flow", pairs)
    return held


def per_device(
    right_side, old_state, block_inverse, flux_jacobian, face_lift, upstream, downstream, live_counts
):
    layers = lax.axis_size("flow")
    rhs = right_side[0]
    elems = rhs.shape[0]
    width = elems // GROUPS
    alive = jnp.arange(elems, dtype=jnp.int32)[:, None] < live_counts[0, 0]
    old = jnp.where(alive, old_state[0], 0.0)
    following = lax.ppermute(old, "flow", [(l + 1, l) for l in range(layers - 1)])
    edge = jnp.pad(old[:1], ((0, 0), (0, WIDE - 320))), jnp.pad(old[-1:], ((0, 0), (0, WIDE - 320)))
    left, right = edge_rows(*edge)
    flux = jnp.transpose(flux_jacobian[0], (2, 1, 0))
    shift = pltpu.VMEM((elems + 16, WIDE), F32)
    cells = jax.ShapeDtypeStruct((elems, WIDE), F32)
    group_cells = (jax.ShapeDtypeStruct((width, WIDE), F32),) * GROUPS
    prep = pltpu.CompilerParams(vmem_limit_bytes=PREP_VMEM)
    *table, up, down, live = pl.pallas_call(
        load_kernel,
        out_shape=(
            jax.ShapeDtypeStruct((elems, 320, 320), BF16),
            jax.ShapeDtypeStruct((elems // 4, 320, 256), BF16),
            jax.ShapeDtypeStruct((4, NVAR, elems, WIDE), F32),
            jax.ShapeDtypeStruct((4, 256, 256), BF16),
            jax.ShapeDtypeStruct((4, 128, 256), BF16),
        ) + (jax.ShapeDtypeStruct((elems, 128), F32),) * 3,
        in_specs=[pl.BlockSpec(memory_space=pltpu.SMEM)] + [ANY_SPEC] * 5,
        out_specs=(VMEM_SPEC,) * 8,
        scratch_shapes=[
            pltpu.VMEM((25, 4, elems), F32),
            pltpu.VMEM((4, NB, NB), F32),
            pltpu.VMEM((2, 1, elems), jnp.int32),
            pltpu.SemaphoreType.DMA((GROUPS + 4,)),
        ],
        compiler_params=prep,
        name="sweep_load",
    )(live_counts, block_inverse[0], flux, face_lift, upstream, downstream)
    mixing = table[2:]
    *fixed, source = pl.pallas_call(
        setup_kernel,
        out_shape=group_cells + (cells,),
        in_specs=[VMEM_SPEC] * 9,
        out_specs=(VMEM_SPEC,) * (GROUPS + 1),
        scratch_shapes=[shift],
        compiler_params=prep,
        name="sweep_setup",
    )(rhs, old, following, left, right, down, *mixing)
    held = sweep(fixed, table, up, live, 0, True, list(range(layers)))
    states = [state for state, _ in held]
    uppers = [upper for _, upper in held]
    left, right = edge_rows(states[0][:1], states[-1][-1:])
    *fixed, half = pl.pallas_call(
        turn_kernel,
        out_shape=group_cells + (jax.ShapeDtypeStruct((elems, 320), F32),),
        in_specs=[VMEM_SPEC] * (6 + 2 * GROUPS),
        out_specs=(VMEM_SPEC,) * (GROUPS + 1),
        scratch_shapes=[shift],
        compiler_params=prep,
        name="sweep_turn",
    )(source, left, right, *mixing, *states, *uppers)
    held = sweep(fixed, table, down, live, 1, False, list(reversed(range(layers))))
    full = pl.pallas_call(
        join_kernel,
        out_shape=jax.ShapeDtypeStruct((elems, 320), F32),
        in_specs=[VMEM_SPEC] * GROUPS,
        out_specs=VMEM_SPEC,
        compiler_params=pltpu.CompilerParams(vmem_limit_bytes=STEP_VMEM),
        name="sweep_join",
    )(*[state for state, in held])
    return half[None], full[None]


def solution(mesh):
    in_specs = (
        P("flow", "cross", None),
        P("flow", "cross", None),
        P("flow", "cross", None, None),
        P("flow", "cross", None, None),
        P(),
        P("flow", "cross"),
        P("flow", "cross"),
        P("flow", "cross"),
    )
    out_specs = (P("flow", "cross", None), P("flow", "cross", None))
    return jax.shard_map(
        per_device, mesh=mesh, in_specs=in_specs, out_specs=out_specs, check_vma=False
    )
```

```python
import functools

import jax
import jax.numpy as jnp
from jax import lax
from jax.experimental import pallas as pl
from jax.experimental.pallas import tpu as pltpu
from jax.sharding import PartitionSpec as P

GROUPS = 4
BLOCK = 8
NVAR = 5
NB = 64
WIDE = 384
ORDER = (0, 3, 1, 2)
SPAN = 4
MIDDLE = 8
STEP_VMEM = 3 << 20
PREP_VMEM = 6 << 20
LOAD_VMEM = 26 << 20

VMEM_SPEC = pl.BlockSpec(memory_space=pltpu.VMEM)
ANY_SPEC = pl.BlockSpec(memory_space=pl.ANY)
HBM_SPEC = pl.BlockSpec(memory_space=pltpu.HBM)
F32 = jnp.float32
BF16 = jnp.bfloat16


def dot(a, b):
    return jnp.dot(a, b, preferred_element_type=jnp.float32)


def split(x):
    high = x.astype(jnp.bfloat16)
    low = (x - high.astype(jnp.float32)).astype(jnp.bfloat16)
    return high, low


def couple(x, lift_high, lift_low, mix):
    m = x.shape[0]
    stacked = jnp.concatenate([x[:, :128], x[:, 128:256], x[:, 256:]], axis=0)
    high, low = split(stacked)
    if lift_low is None:
        spread = dot(high, lift_high[:128])
    else:
        spread = dot(jnp.concatenate([high, low], axis=1), lift_high) + dot(high, lift_low)
    parts = [spread[v // 2 * m : v // 2 * m + m, v % 2 * 128 : v % 2 * 128 + 128] for v in range(NVAR)]
    chunks = []
    for k in range(3):
        at = slice(128 * k, 128 * k + 128)
        total = mix[0][:, at] * parts[0]
        for v in range(1, NVAR):
            total = total + mix[v][:, at] * parts[v]
        chunks.append(total)
    return jnp.concatenate(chunks, axis=1)


def padded(x):
    return jnp.concatenate([x, jnp.zeros((x.shape[0], WIDE - x.shape[1]), x.dtype)], axis=1)


def dot_t(a, b):
    return lax.dot_general(a, b, (((1,), (1,)), ((), ())), preferred_element_type=F32)


def gathered(x, delta):
    rows = x.shape[0]
    cells = x.reshape(rows // 8, 8, x.shape[1])
    chunks = []
    for k in range(3):
        chunk = cells[:, :, 128 * k : 128 * k + 128]
        moved = chunk
        for d in (-3, -2, -1, 1, 2, 3):
            moved = jnp.where(delta.reshape(rows // 8, 8, 128) == d, pltpu.roll(chunk, (-d) % 8, 1), moved)
        chunks.append(moved.reshape(rows, 128))
    return jnp.concatenate(chunks, axis=1)


def load_kernel(
    count_ref, inverse_ref, flux_ref, lift_hbm, up_ref, down_ref,
    main_ref, rem_ref, mix_ref, high_ref, low_ref, up_out, down_out, live_ref,
    flux_buf, lift_ref, slots, sems,
):
    elems = main_ref.shape[0]
    width = elems // GROUPS
    small = [
        pltpu.make_async_copy(src, dst, sems.at[GROUPS + n])
        for n, (src, dst) in enumerate(
            [(flux_ref, flux_buf), (lift_hbm, lift_ref), (up_ref, slots.at[0]), (down_ref, slots.at[1])]
        )
    ]
    large = []
    for p in range(GROUPS):
        rows = pl.ds(p * width, width)
        large.append(pltpu.make_async_copy(inverse_ref.at[rows], main_ref.at[rows], sems.at[p]))
    for copy in small + large:
        copy.start()
    for copy in small:
        copy.wait()
    row = lax.broadcasted_iota(jnp.int32, (elems, 128), 0)
    for n, out in enumerate((up_out, down_out)):
        local = (slots[n] & (elems - 1)).astype(F32)
        out[...] = jnp.broadcast_to(local, (128, elems)).T - row.astype(F32)
    live_ref[...] = jnp.where(row < count_ref[0, 0], 1.0, 0.0)
    lane = lax.broadcasted_iota(jnp.int32, (elems, 128), 1)
    for d in range(4):
        lift_t = lift_ref[d].T
        both = jnp.concatenate([lift_t, lift_t], axis=1)
        none = jnp.zeros_like(both)
        weight = jnp.concatenate(
            [jnp.concatenate([both, none], axis=1), jnp.concatenate([none, both], axis=1)], axis=0
        )
        high, low = split(weight)
        high_ref[d] = jnp.concatenate([high, high], axis=0)
        low_ref[d] = low
        flux = flux_buf[:, d, :]
        flux = jnp.concatenate([flux, jnp.zeros((7, elems), F32)], axis=0).T
        for v in range(NVAR):
            for k in range(3):
                u = 2 * k
                first = jnp.broadcast_to(flux[:, 5 * u + v : 5 * u + v + 1], (elems, 128))
                if u + 1 < NVAR:
                    at = 5 * (u + 1) + v
                    second = jnp.broadcast_to(flux[:, at : at + 1], (elems, 128))
                else:
                    second = jnp.zeros((elems, 128), F32)
                mix_ref[d, v, :, 128 * k : 128 * k + 128] = jnp.where(lane < NB, first, second)
    for p in range(GROUPS):
        large[p].wait()

        @pl.loop(p * width // 4, (p + 1) * width // 4)
        def _(q):
            rem_ref[q] = jnp.concatenate([main_ref[4 * q + j, :, 256:320] for j in range(4)], axis=1)


def face_of(x, d, mix_ref, high_ref, low_ref):
    return couple(x, high_ref[d], low_ref[d], [mix_ref[d, v] for v in range(NVAR)])


def beside(shift_ref, left_ref, right_ref):
    elems = shift_ref.shape[0] - 16
    shift_ref[7:8, :] = left_ref[...]
    shift_ref[elems + 8 : elems + 9, :] = right_ref[...]
    return shift_ref[7 : elems + 7, :], shift_ref[9 : elems + 9, :]


def put_groups(fixed, refs):
    width = refs[0].shape[0]
    for p, ref in enumerate(refs):
        ref[...] = fixed[p * width : p * width + width]


def setup_kernel(
    rhs_ref, old_ref, next_ref, left_ref, right_ref, delta_ref, mix_ref, high_ref, low_ref, *refs
):
    fixed_refs, (source_ref, shift_ref) = refs[:GROUPS], refs[GROUPS:]
    elems = rhs_ref.shape[0]
    source = padded(rhs_ref[...])
    source_ref[...] = source
    shift_ref[8 : elems + 8, :] = padded(old_ref[...])
    before, after = beside(shift_ref, left_ref, right_ref)
    below = gathered(padded(next_ref[...]), delta_ref[...])
    fixed = source - face_of(below, 1, mix_ref, high_ref, low_ref)
    fixed = fixed - face_of(before, 2, mix_ref, high_ref, low_ref)
    put_groups(fixed - face_of(after, 3, mix_ref, high_ref, low_ref), fixed_refs)


def turn_kernel(source_ref, left_ref, right_ref, mix_ref, high_ref, low_ref, *refs):
    states, uppers = refs[:GROUPS], refs[GROUPS : 2 * GROUPS]
    fixed_refs, (half_ref, shift_ref) = refs[2 * GROUPS : 3 * GROUPS], refs[3 * GROUPS :]
    width = states[0].shape[0]
    for p in range(GROUPS):
        shift_ref[8 + p * width : 8 + p * width + width, :] = states[p][...]
        half_ref[p * width : p * width + width, :] = states[p][:, :320]
    before, after = beside(shift_ref, left_ref, right_ref)
    fixed = source_ref[...] - jnp.concatenate([upper[...] for upper in uppers], axis=0)
    fixed = fixed - face_of(before, 2, mix_ref, high_ref, low_ref)
    put_groups(fixed - face_of(after, 3, mix_ref, high_ref, low_ref), fixed_refs)


def join_kernel(*refs):
    width = refs[0].shape[0]
    for p in range(GROUPS):
        refs[GROUPS][p * width : p * width + width, :] = refs[p][:, :320]


def step_kernel(
    layer, face, group, keep, flipped,
    message_ref, main_ref, rem_ref, fixed_ref, mix_ref, high_ref, delta_ref, live_ref,
    token_ref, *refs,
):
    del token_ref
    count = 2 if keep else 1
    held_refs, new_refs, (body_ref,) = refs[:count], refs[count : 2 * count], refs[2 * count :]
    width = message_ref.shape[0]
    active = lax.axis_index("flow") == layer

    @pl.when(active)
    def _():
        base = group * width
        rows = pl.ds(base, width)
        mix = [mix_ref[face, v, rows, :] for v in range(NVAR)]
        inflow = couple(gathered(message_ref[...], delta_ref[rows, :]), high_ref[face], None, mix)
        if keep:
            new_refs[1][...] = inflow
        resid = fixed_ref[...] - inflow
        tail = resid[:, 256:]
        tail = tail + pltpu.roll(tail, 64, 1)
        row = lax.broadcasted_iota(jnp.int32, (width, 256), 0)
        lane = lax.broadcasted_iota(jnp.int32, (width, 256), 1)
        body_ref[:, :256] = resid[:, :256]
        body_ref[:, 256:] = jnp.where(row % 4 == lane // 64, jnp.concatenate([tail, tail], axis=1), 0.0)
        at = lax.broadcasted_iota(jnp.int32, (BLOCK, 320), 0)

        @pl.loop(0, width // BLOCK)
        def _(b):
            part = pl.ds(pl.multiple_of(b * BLOCK, BLOCK), BLOCK)
            both = body_ref[part, :].astype(BF16)
            first = base + b * BLOCK
            rest = jnp.zeros((BLOCK, 320), F32)
            solved = jnp.zeros((BLOCK, 320), F32)
            times = dot if flipped else dot_t
            for q in range(BLOCK // 4):
                rest = jnp.where(at // 4 == q, times(both[:, 256:], rem_ref[first // 4 + q]), rest)
                for e in range(4 * q, 4 * q + 4):
                    block = main_ref[first + e] if flipped else main_ref[first + e, :, :256]
                    solved = jnp.where(at == e, times(both[:, :256], block), solved)
            wide = padded(solved + rest)
            live = live_ref[pl.ds(pl.multiple_of(first, BLOCK), BLOCK), :]
            wide = wide * jnp.concatenate([live, live, live], axis=1)
            new_refs[0][part, :] = wide

    @pl.when(jnp.logical_not(active))
    def _():
        for held, new in zip(held_refs, new_refs):
            new[...] = held[...]


def flip_kernel(low, high, inverse_ref, token_ref, *refs):
    main_ref, rem_ref, done_ref = refs[-3:]
    place = lax.axis_index("flow")
    done_ref[...] = jnp.zeros_like(done_ref)

    @pl.when((place >= low) & (place < high))
    def _():
        @pl.loop(0, inverse_ref.shape[0] // 4)
        def _(q):
            for j in range(4):
                turned = inverse_ref[4 * q + j].T
                main_ref[4 * q + j] = turned[:256]
                rem_ref[q, 64 * j : 64 * j + 64, :] = turned[256:]


def flip_call(inverse, token, earlier, low, high):
    elems = inverse.shape[0]
    return pl.pallas_call(
        functools.partial(flip_kernel, low, high),
        out_shape=(
            jax.ShapeDtypeStruct((elems, 256, 320), BF16),
            jax.ShapeDtypeStruct((elems // 4, 256, 320), BF16),
            jax.ShapeDtypeStruct((8, 128), F32),
        ),
        in_specs=[VMEM_SPEC, ANY_SPEC] + [VMEM_SPEC] * len(earlier),
        out_specs=(VMEM_SPEC,) * 3,
        input_output_aliases={2 + n: n for n in range(len(earlier))},
        compiler_params=pltpu.CompilerParams(vmem_limit_bytes=STEP_VMEM),
        name="sweep_flip",
    )(inverse, token, *earlier)


def step_call(layer, face, group, keep, flipped, width):
    body = functools.partial(step_kernel, layer, face, group, keep, flipped)
    count = 2 if keep else 1
    cells = jax.ShapeDtypeStruct((width, WIDE), F32)
    return pl.pallas_call(
        body,
        out_shape=(cells,) * count,
        in_specs=[VMEM_SPEC] * 8 + [ANY_SPEC] + [VMEM_SPEC] * count,
        out_specs=(VMEM_SPEC,) * count,
        scratch_shapes=[pltpu.VMEM((width, 512), F32)],
        compiler_params=pltpu.CompilerParams(
            vmem_limit_bytes=STEP_VMEM
        ),
        cost_estimate=pl.CostEstimate(flops=width * 320 * 320 * 2, bytes_accessed=width * 320 * 320 * 2, transcendentals=0),
        name="sweep_step",
    )


def edge_rows(first, last):
    count = lax.axis_size("cross")
    right = [(i, i + 1) for i in range(count - 1)]
    left = [(i + 1, i) for i in range(count - 1)]
    return lax.ppermute(last, "cross", right), lax.ppermute(first, "cross", left)


def sweep(fixed, table, flips, delta, live, face, keep, route):
    width = fixed[0].shape[0]
    blank = jnp.zeros((width, WIDE), F32)
    messages = [blank] * GROUPS
    held = [(blank,) * (2 if keep else 1)] * GROUPS
    token = fixed[0]
    last = len(route) - 1
    for i, layer in enumerate(route):
        for p in ORDER:
            flipped = len(flips) == 2
            call = step_call(layer, face, p, keep, flipped, width)
            main, rem, mix, high = table[:4]
            if flipped:
                main, rem = flips[1]
            new = call(messages[p], main, rem, fixed[p], mix, high, delta, live, token, *held[p])
            token = new[0]
            held[p] = tuple(new)
            if i < last:
                pairs = [(route[k], route[k + 1]) for k in range(i % SPAN, last, SPAN)]
                messages[p] = lax.ppermute(token, "flow", pairs)
        if keep and i == 0:
            *flip, token = flip_call(table[0], token, (), MIDDLE, len(route))
            flips.append(flip)
        if keep and i == MIDDLE + 1:
            *flip, token = flip_call(table[0], token, flips[0], 0, MIDDLE)
            flips.append(flip)
    return held


def per_device(
    right_side, old_state, block_inverse, flux_jacobian, face_lift, upstream, downstream, live_counts
):
    layers = lax.axis_size("flow")
    rhs = right_side[0]
    elems = rhs.shape[0]
    width = elems // GROUPS
    alive = jnp.arange(elems, dtype=jnp.int32)[:, None] < live_counts[0, 0]
    old = jnp.where(alive, old_state[0], 0.0)
    following = lax.ppermute(old, "flow", [(l + 1, l) for l in range(layers - 1)])
    edge = jnp.pad(old[:1], ((0, 0), (0, WIDE - 320))), jnp.pad(old[-1:], ((0, 0), (0, WIDE - 320)))
    left, right = edge_rows(*edge)
    flux = jnp.transpose(flux_jacobian[0], (2, 1, 0))
    shift = pltpu.VMEM((elems + 16, WIDE), F32)
    cells = jax.ShapeDtypeStruct((elems, WIDE), F32)
    group_cells = (jax.ShapeDtypeStruct((width, WIDE), F32),) * GROUPS
    prep = pltpu.CompilerParams(vmem_limit_bytes=PREP_VMEM)
    *table, up, down, live = pl.pallas_call(
        load_kernel,
        out_shape=(
            jax.ShapeDtypeStruct((elems, 320, 320), BF16),
            jax.ShapeDtypeStruct((elems // 4, 320, 256), BF16),
            jax.ShapeDtypeStruct((4, NVAR, elems, WIDE), F32),
            jax.ShapeDtypeStruct((4, 256, 256), BF16),
            jax.ShapeDtypeStruct((4, 128, 256), BF16),
        ) + (jax.ShapeDtypeStruct((elems, 128), F32),) * 3,
        in_specs=[pl.BlockSpec(memory_space=pltpu.SMEM)] + [HBM_SPEC] * 5,
        out_specs=(VMEM_SPEC,) * 8,
        scratch_shapes=[
            pltpu.VMEM((25, 4, elems), F32),
            pltpu.VMEM((4, NB, NB), F32),
            pltpu.VMEM((2, 1, elems), jnp.int32),
            pltpu.SemaphoreType.DMA((GROUPS + 4,)),
        ],
        compiler_params=pltpu.CompilerParams(vmem_limit_bytes=LOAD_VMEM),
        name="sweep_load",
    )(live_counts, block_inverse[0], flux, face_lift, upstream, downstream)
    mixing = table[2:]
    *fixed, source = pl.pallas_call(
        setup_kernel,
        out_shape=group_cells + (cells,),
        in_specs=[VMEM_SPEC] * 9,
        out_specs=(VMEM_SPEC,) * (GROUPS + 1),
        scratch_shapes=[shift],
        compiler_params=prep,
        name="sweep_setup",
    )(rhs, old, following, left, right, down, *mixing)
    flips = []
    held = sweep(fixed, table, flips, up, live, 0, True, list(range(layers)))
    states = [state for state, _ in held]
    uppers = [upper for _, upper in held]
    left, right = edge_rows(states[0][:1], states[-1][-1:])
    *fixed, half = pl.pallas_call(
        turn_kernel,
        out_shape=group_cells + (jax.ShapeDtypeStruct((elems, 320), F32),),
        in_specs=[VMEM_SPEC] * (6 + 2 * GROUPS),
        out_specs=(VMEM_SPEC,) * (GROUPS + 1),
        scratch_shapes=[shift],
        compiler_params=prep,
        name="sweep_turn",
    )(source, left, right, *mixing, *states, *uppers)
    held = sweep(fixed, table, flips, down, live, 1, False, list(reversed(range(layers))))
    full = pl.pallas_call(
        join_kernel,
        out_shape=jax.ShapeDtypeStruct((elems, 320), F32),
        in_specs=[VMEM_SPEC] * GROUPS,
        out_specs=VMEM_SPEC,
        compiler_params=pltpu.CompilerParams(vmem_limit_bytes=STEP_VMEM),
        name="sweep_join",
    )(*[state for state, in held])
    return half[None], full[None]


def solution(mesh):
    in_specs = (
        P("flow", "cross", None),
        P("flow", "cross", None),
        P("flow", "cross", None, None),
        P("flow", "cross", None, None),
        P(),
        P("flow", "cross"),
        P("flow", "cross"),
        P("flow", "cross"),
    )
    out_specs = (P("flow", "cross", None), P("flow", "cross", None))
    return jax.shard_map(
        per_device, mesh=mesh, in_specs=in_specs, out_specs=out_specs, check_vma=False
    )
```

```python
import functools

import jax
import jax.numpy as jnp
from jax import lax
from jax.experimental import pallas as pl
from jax.experimental.pallas import tpu as pltpu
from jax.sharding import PartitionSpec as P

GROUPS = 4
BLOCK = 8
NVAR = 5
NB = 64
WIDE = 384
ORDER = (0, 3, 1, 2)
SPAN = 4
MIDDLE = 10
STEP_VMEM = 3 << 20
PREP_VMEM = 6 << 20
LOAD_VMEM = 26 << 20

VMEM_SPEC = pl.BlockSpec(memory_space=pltpu.VMEM)
ANY_SPEC = pl.BlockSpec(memory_space=pl.ANY)
HBM_SPEC = pl.BlockSpec(memory_space=pltpu.HBM)
F32 = jnp.float32
BF16 = jnp.bfloat16


def dot(a, b):
    return jnp.dot(a, b, preferred_element_type=jnp.float32)


def split(x):
    high = x.astype(jnp.bfloat16)
    low = (x - high.astype(jnp.float32)).astype(jnp.bfloat16)
    return high, low


def couple(x, lift_high, lift_low, mix):
    m = x.shape[0]
    stacked = jnp.concatenate([x[:, :128], x[:, 128:256], x[:, 256:]], axis=0)
    high, low = split(stacked)
    if lift_low is None:
        spread = dot(high, lift_high[:128])
    else:
        spread = dot(jnp.concatenate([high, low], axis=1), lift_high) + dot(high, lift_low)
    parts = [spread[v // 2 * m : v // 2 * m + m, v % 2 * 128 : v % 2 * 128 + 128] for v in range(NVAR)]
    chunks = []
    for k in range(3):
        at = slice(128 * k, 128 * k + 128)
        total = mix[0][:, at] * parts[0]
        for v in range(1, NVAR):
            total = total + mix[v][:, at] * parts[v]
        chunks.append(total)
    return jnp.concatenate(chunks, axis=1)


def padded(x):
    return jnp.concatenate([x, jnp.zeros((x.shape[0], WIDE - x.shape[1]), x.dtype)], axis=1)


def dot_t(a, b):
    return lax.dot_general(a, b, (((1,), (1,)), ((), ())), preferred_element_type=F32)


def gathered(x, delta):
    rows = x.shape[0]
    cells = x.reshape(rows // 8, 8, x.shape[1])
    chunks = []
    for k in range(3):
        chunk = cells[:, :, 128 * k : 128 * k + 128]
        moved = chunk
        for d in (-3, -2, -1, 1, 2, 3):
            moved = jnp.where(delta.reshape(rows // 8, 8, 128) == d, pltpu.roll(chunk, (-d) % 8, 1), moved)
        chunks.append(moved.reshape(rows, 128))
    return jnp.concatenate(chunks, axis=1)


def load_kernel(
    count_ref, inverse_ref, flux_ref, lift_hbm, up_ref, down_ref,
    main_ref, rem_ref, mix_ref, high_ref, low_ref, up_out, down_out, live_ref,
    flux_buf, lift_ref, slots, sems,
):
    elems = main_ref.shape[0]
    width = elems // GROUPS
    small = [
        pltpu.make_async_copy(src, dst, sems.at[GROUPS + n])
        for n, (src, dst) in enumerate(
            [(flux_ref, flux_buf), (lift_hbm, lift_ref), (up_ref, slots.at[0]), (down_ref, slots.at[1])]
        )
    ]
    large = []
    for p in range(GROUPS):
        rows = pl.ds(p * width, width)
        large.append(pltpu.make_async_copy(inverse_ref.at[rows], main_ref.at[rows], sems.at[p]))
    for copy in small + large:
        copy.start()
    for copy in small:
        copy.wait()
    row = lax.broadcasted_iota(jnp.int32, (elems, 128), 0)
    for n, out in enumerate((up_out, down_out)):
        local = (slots[n] & (elems - 1)).astype(F32)
        out[...] = jnp.broadcast_to(local, (128, elems)).T - row.astype(F32)
    live_ref[...] = jnp.where(row < count_ref[0, 0], 1.0, 0.0)
    lane = lax.broadcasted_iota(jnp.int32, (elems, 128), 1)
    for d in range(4):
        lift_t = lift_ref[d].T
        both = jnp.concatenate([lift_t, lift_t], axis=1)
        none = jnp.zeros_like(both)
        weight = jnp.concatenate(
            [jnp.concatenate([both, none], axis=1), jnp.concatenate([none, both], axis=1)], axis=0
        )
        high, low = split(weight)
        high_ref[d] = jnp.concatenate([high, high], axis=0)
        low_ref[d] = low
        flux = flux_buf[:, d, :]
        flux = jnp.concatenate([flux, jnp.zeros((7, elems), F32)], axis=0).T
        for v in range(NVAR):
            for k in range(3):
                u = 2 * k
                first = jnp.broadcast_to(flux[:, 5 * u + v : 5 * u + v + 1], (elems, 128))
                if u + 1 < NVAR:
                    at = 5 * (u + 1) + v
                    second = jnp.broadcast_to(flux[:, at : at + 1], (elems, 128))
                else:
                    second = jnp.zeros((elems, 128), F32)
                mix_ref[d, v, :, 128 * k : 128 * k + 128] = jnp.where(lane < NB, first, second)
    for p in range(GROUPS):
        large[p].wait()

        @pl.loop(p * width // 4, (p + 1) * width // 4)
        def _(q):
            rem_ref[q] = jnp.concatenate([main_ref[4 * q + j, :, 256:320] for j in range(4)], axis=1)


def face_of(x, d, mix_ref, high_ref, low_ref):
    return couple(x, high_ref[d], low_ref[d], [mix_ref[d, v] for v in range(NVAR)])


def beside(shift_ref, left_ref, right_ref):
    elems = shift_ref.shape[0] - 16
    shift_ref[7:8, :] = left_ref[...]
    shift_ref[elems + 8 : elems + 9, :] = right_ref[...]
    return shift_ref[7 : elems + 7, :], shift_ref[9 : elems + 9, :]


def put_groups(fixed, refs):
    width = refs[0].shape[0]
    for p, ref in enumerate(refs):
        ref[...] = fixed[p * width : p * width + width]


def setup_kernel(
    rhs_ref, old_ref, next_ref, left_ref, right_ref, delta_ref, mix_ref, high_ref, low_ref, *refs
):
    fixed_refs, (source_ref, shift_ref) = refs[:GROUPS], refs[GROUPS:]
    elems = rhs_ref.shape[0]
    source = padded(rhs_ref[...])
    source_ref[...] = source
    shift_ref[8 : elems + 8, :] = padded(old_ref[...])
    before, after = beside(shift_ref, left_ref, right_ref)
    below = gathered(padded(next_ref[...]), delta_ref[...])
    fixed = source - face_of(below, 1, mix_ref, high_ref, low_ref)
    fixed = fixed - face_of(before, 2, mix_ref, high_ref, low_ref)
    put_groups(fixed - face_of(after, 3, mix_ref, high_ref, low_ref), fixed_refs)


def turn_kernel(source_ref, left_ref, right_ref, mix_ref, high_ref, low_ref, *refs):
    states, uppers = refs[:GROUPS], refs[GROUPS : 2 * GROUPS]
    fixed_refs, (half_ref, shift_ref) = refs[2 * GROUPS : 3 * GROUPS], refs[3 * GROUPS :]
    width = states[0].shape[0]
    for p in range(GROUPS):
        shift_ref[8 + p * width : 8 + p * width + width, :] = states[p][...]
        half_ref[p * width : p * width + width, :] = states[p][:, :320]
    before, after = beside(shift_ref, left_ref, right_ref)
    fixed = source_ref[...] - jnp.concatenate([upper[...] for upper in uppers], axis=0)
    fixed = fixed - face_of(before, 2, mix_ref, high_ref, low_ref)
    put_groups(fixed - face_of(after, 3, mix_ref, high_ref, low_ref), fixed_refs)


def join_kernel(*refs):
    width = refs[0].shape[0]
    for p in range(GROUPS):
        refs[GROUPS][p * width : p * width + width, :] = refs[p][:, :320]


def step_kernel(
    layer, face, group, keep, flipped,
    message_ref, main_ref, rem_ref, fixed_ref, mix_ref, high_ref, delta_ref, live_ref,
    token_ref, *refs,
):
    del token_ref
    count = 2 if keep else 1
    held_refs, new_refs, (body_ref,) = refs[:count], refs[count : 2 * count], refs[2 * count :]
    width = message_ref.shape[0]
    active = lax.axis_index("flow") == layer

    @pl.when(active)
    def _():
        base = group * width
        rows = pl.ds(base, width)
        mix = [mix_ref[face, v, rows, :] for v in range(NVAR)]
        inflow = couple(gathered(message_ref[...], delta_ref[rows, :]), high_ref[face], None, mix)
        if keep:
            new_refs[1][...] = inflow
        resid = fixed_ref[...] - inflow
        tail = resid[:, 256:]
        tail = tail + pltpu.roll(tail, 64, 1)
        row = lax.broadcasted_iota(jnp.int32, (width, 256), 0)
        lane = lax.broadcasted_iota(jnp.int32, (width, 256), 1)
        body_ref[:, :256] = resid[:, :256]
        body_ref[:, 256:] = jnp.where(row % 4 == lane // 64, jnp.concatenate([tail, tail], axis=1), 0.0)
        at = lax.broadcasted_iota(jnp.int32, (BLOCK, 320), 0)

        @pl.loop(0, width // BLOCK)
        def _(b):
            part = pl.ds(pl.multiple_of(b * BLOCK, BLOCK), BLOCK)
            both = body_ref[part, :].astype(BF16)
            first = base + b * BLOCK
            rest = jnp.zeros((BLOCK, 320), F32)
            solved = jnp.zeros((BLOCK, 320), F32)
            times = dot if flipped else dot_t
            for q in range(BLOCK // 4):
                rest = jnp.where(at // 4 == q, times(both[:, 256:], rem_ref[first // 4 + q]), rest)
                for e in range(4 * q, 4 * q + 4):
                    block = main_ref[first + e] if flipped else main_ref[first + e, :, :256]
                    solved = jnp.where(at == e, times(both[:, :256], block), solved)
            wide = padded(solved + rest)
            live = live_ref[pl.ds(pl.multiple_of(first, BLOCK), BLOCK), :]
            wide = wide * jnp.concatenate([live, live, live], axis=1)
            new_refs[0][part, :] = wide

    @pl.when(jnp.logical_not(active))
    def _():
        for held, new in zip(held_refs, new_refs):
            new[...] = held[...]


def flip_kernel(low, high, inverse_ref, token_ref, *refs):
    main_ref, rem_ref, done_ref = refs[-3:]
    place = lax.axis_index("flow")
    done_ref[...] = jnp.zeros_like(done_ref)

    @pl.when((place >= low) & (place < high))
    def _():
        @pl.loop(0, inverse_ref.shape[0] // 4)
        def _(q):
            for j in range(4):
                turned = inverse_ref[4 * q + j].T
                main_ref[4 * q + j] = turned[:256]
                rem_ref[q, 64 * j : 64 * j + 64, :] = turned[256:]


def flip_call(inverse, token, earlier, low, high):
    elems = inverse.shape[0]
    return pl.pallas_call(
        functools.partial(flip_kernel, low, high),
        out_shape=(
            jax.ShapeDtypeStruct((elems, 256, 320), BF16),
            jax.ShapeDtypeStruct((elems // 4, 256, 320), BF16),
            jax.ShapeDtypeStruct((8, 128), F32),
        ),
        in_specs=[VMEM_SPEC, ANY_SPEC] + [VMEM_SPEC] * len(earlier),
        out_specs=(VMEM_SPEC,) * 3,
        input_output_aliases={2 + n: n for n in range(len(earlier))},
        compiler_params=pltpu.CompilerParams(vmem_limit_bytes=STEP_VMEM),
        name="sweep_flip",
    )(inverse, token, *earlier)


def step_call(layer, face, group, keep, flipped, width):
    body = functools.partial(step_kernel, layer, face, group, keep, flipped)
    count = 2 if keep else 1
    cells = jax.ShapeDtypeStruct((width, WIDE), F32)
    return pl.pallas_call(
        body,
        out_shape=(cells,) * count,
        in_specs=[VMEM_SPEC] * 8 + [ANY_SPEC] + [VMEM_SPEC] * count,
        out_specs=(VMEM_SPEC,) * count,
        scratch_shapes=[pltpu.VMEM((width, 512), F32)],
        compiler_params=pltpu.CompilerParams(
            vmem_limit_bytes=STEP_VMEM
        ),
        cost_estimate=pl.CostEstimate(flops=width * 320 * 320 * 2, bytes_accessed=width * 320 * 320 * 2, transcendentals=0),
        name="sweep_step",
    )


def edge_rows(first, last):
    count = lax.axis_size("cross")
    right = [(i, i + 1) for i in range(count - 1)]
    left = [(i + 1, i) for i in range(count - 1)]
    return lax.ppermute(last, "cross", right), lax.ppermute(first, "cross", left)


def sweep(fixed, table, flips, delta, live, face, keep, route):
    width = fixed[0].shape[0]
    blank = jnp.zeros((width, WIDE), F32)
    messages = [blank] * GROUPS
    held = [(blank,) * (2 if keep else 1)] * GROUPS
    token = fixed[0]
    last = len(route) - 1
    for i, layer in enumerate(route):
        for p in ORDER:
            flipped = len(flips) == 2
            call = step_call(layer, face, p, keep, flipped, width)
            main, rem, mix, high = table[:4]
            if flipped:
                main, rem = flips[1]
            new = call(messages[p], main, rem, fixed[p], mix, high, delta, live, token, *held[p])
            token = new[0]
            held[p] = tuple(new)
            if i < last:
                pairs = [(route[k], route[k + 1]) for k in range(i % SPAN, last, SPAN)]
                messages[p] = lax.ppermute(token, "flow", pairs)
        if keep and i == 0:
            *flip, token = flip_call(table[0], token, (), MIDDLE, len(route))
            flips.append(flip)
        if keep and i == MIDDLE + 1:
            *flip, token = flip_call(table[0], token, flips[0], 0, MIDDLE)
            flips.append(flip)
    return held


def per_device(
    right_side, old_state, block_inverse, flux_jacobian, face_lift, upstream, downstream, live_counts
):
    layers = lax.axis_size("flow")
    rhs = right_side[0]
    elems = rhs.shape[0]
    width = elems // GROUPS
    alive = jnp.arange(elems, dtype=jnp.int32)[:, None] < live_counts[0, 0]
    old = jnp.where(alive, old_state[0], 0.0)
    following = lax.ppermute(old, "flow", [(l + 1, l) for l in range(layers - 1)])
    edge = jnp.pad(old[:1], ((0, 0), (0, WIDE - 320))), jnp.pad(old[-1:], ((0, 0), (0, WIDE - 320)))
    left, right = edge_rows(*edge)
    flux = jnp.transpose(flux_jacobian[0], (2, 1, 0))
    shift = pltpu.VMEM((elems + 16, WIDE), F32)
    cells = jax.ShapeDtypeStruct((elems, WIDE), F32)
    group_cells = (jax.ShapeDtypeStruct((width, WIDE), F32),) * GROUPS
    prep = pltpu.CompilerParams(vmem_limit_bytes=PREP_VMEM)
    *table, up, down, live = pl.pallas_call(
        load_kernel,
        out_shape=(
            jax.ShapeDtypeStruct((elems, 320, 320), BF16),
            jax.ShapeDtypeStruct((elems // 4, 320, 256), BF16),
            jax.ShapeDtypeStruct((4, NVAR, elems, WIDE), F32),
            jax.ShapeDtypeStruct((4, 256, 256), BF16),
            jax.ShapeDtypeStruct((4, 128, 256), BF16),
        ) + (jax.ShapeDtypeStruct((elems, 128), F32),) * 3,
        in_specs=[pl.BlockSpec(memory_space=pltpu.SMEM)] + [HBM_SPEC] * 5,
        out_specs=(VMEM_SPEC,) * 8,
        scratch_shapes=[
            pltpu.VMEM((25, 4, elems), F32),
            pltpu.VMEM((4, NB, NB), F32),
            pltpu.VMEM((2, 1, elems), jnp.int32),
            pltpu.SemaphoreType.DMA((GROUPS + 4,)),
        ],
        compiler_params=pltpu.CompilerParams(vmem_limit_bytes=LOAD_VMEM),
        name="sweep_load",
    )(live_counts, *[
        pltpu.with_memory_space_constraint(x, pltpu.HBM)
        for x in (block_inverse[0], flux, face_lift, upstream, downstream)
    ])
    mixing = table[2:]
    *fixed, source = pl.pallas_call(
        setup_kernel,
        out_shape=group_cells + (cells,),
        in_specs=[VMEM_SPEC] * 9,
        out_specs=(VMEM_SPEC,) * (GROUPS + 1),
        scratch_shapes=[shift],
        compiler_params=prep,
        name="sweep_setup",
    )(rhs, old, following, left, right, down, *mixing)
    flips = []
    held = sweep(fixed, table, flips, up, live, 0, True, list(range(layers)))
    states = [state for state, _ in held]
    uppers = [upper for _, upper in held]
    left, right = edge_rows(states[0][:1], states[-1][-1:])
    *fixed, half = pl.pallas_call(
        turn_kernel,
        out_shape=group_cells + (jax.ShapeDtypeStruct((elems, 320), F32),),
        in_specs=[VMEM_SPEC] * (6 + 2 * GROUPS),
        out_specs=(VMEM_SPEC,) * (GROUPS + 1),
        scratch_shapes=[shift],
        compiler_params=prep,
        name="sweep_turn",
    )(source, left, right, *mixing, *states, *uppers)
    held = sweep(fixed, table, flips, down, live, 1, False, list(reversed(range(layers))))
    full = pl.pallas_call(
        join_kernel,
        out_shape=jax.ShapeDtypeStruct((elems, 320), F32),
        in_specs=[VMEM_SPEC] * GROUPS,
        out_specs=VMEM_SPEC,
        compiler_params=pltpu.CompilerParams(vmem_limit_bytes=STEP_VMEM),
        name="sweep_join",
    )(*[state for state, in held])
    return half[None], full[None]


def solution(mesh):
    in_specs = (
        P("flow", "cross", None),
        P("flow", "cross", None),
        P("flow", "cross", None, None),
        P("flow", "cross", None, None),
        P(),
        P("flow", "cross"),
        P("flow", "cross"),
        P("flow", "cross"),
    )
    out_specs = (P("flow", "cross", None), P("flow", "cross", None))
    return jax.shard_map(
        per_device, mesh=mesh, in_specs=in_specs, out_specs=out_specs, check_vma=False
    )
```

```python
import functools

import jax
import jax.numpy as jnp
from jax import lax
from jax.experimental import pallas as pl
from jax.experimental.pallas import tpu as pltpu
from jax.sharding import PartitionSpec as P

GROUPS = 4
BLOCK = 8
NVAR = 5
NB = 64
WIDE = 384
ORDER = (0, 3, 1, 2)
SPAN = 4
MIDDLE = 10
STEP_VMEM = 3 << 20
PREP_VMEM = 6 << 20
LOAD_VMEM = 26 << 20

VMEM_SPEC = pl.BlockSpec(memory_space=pltpu.VMEM)
ANY_SPEC = pl.BlockSpec(memory_space=pl.ANY)
HBM_SPEC = pl.BlockSpec(memory_space=pltpu.HBM)
F32 = jnp.float32
BF16 = jnp.bfloat16


def dot(a, b):
    return jnp.dot(a, b, preferred_element_type=jnp.float32)


def split(x):
    high = x.astype(jnp.bfloat16)
    low = (x - high.astype(jnp.float32)).astype(jnp.bfloat16)
    return high, low


def couple(x, lift_high, lift_low, mix):
    m = x.shape[0]
    stacked = jnp.concatenate([x[:, :128], x[:, 128:256], x[:, 256:]], axis=0)
    high, low = split(stacked)
    if lift_low is None:
        spread = dot(high, lift_high[:128])
    else:
        spread = dot(jnp.concatenate([high, low], axis=1), lift_high) + dot(high, lift_low)
    parts = [spread[v // 2 * m : v // 2 * m + m, v % 2 * 128 : v % 2 * 128 + 128] for v in range(NVAR)]
    chunks = []
    for k in range(3):
        at = slice(128 * k, 128 * k + 128)
        total = mix[0][:, at] * parts[0]
        for v in range(1, NVAR):
            total = total + mix[v][:, at] * parts[v]
        chunks.append(total)
    return jnp.concatenate(chunks, axis=1)


def padded(x):
    return jnp.concatenate([x, jnp.zeros((x.shape[0], WIDE - x.shape[1]), x.dtype)], axis=1)


def dot_t(a, b):
    return lax.dot_general(a, b, (((1,), (1,)), ((), ())), preferred_element_type=F32)


def gathered(x, delta):
    rows = x.shape[0]
    cells = x.reshape(rows // 8, 8, x.shape[1])
    chunks = []
    for k in range(3):
        chunk = cells[:, :, 128 * k : 128 * k + 128]
        moved = chunk
        for d in (-3, -2, -1, 1, 2, 3):
            moved = jnp.where(delta.reshape(rows // 8, 8, 128) == d, pltpu.roll(chunk, (-d) % 8, 1), moved)
        chunks.append(moved.reshape(rows, 128))
    return jnp.concatenate(chunks, axis=1)


def load_kernel(
    count_ref, inverse_ref, flux_ref, lift_hbm, up_ref, down_ref,
    main_ref, rem_ref, mix_ref, high_ref, low_ref, up_out, down_out, live_ref,
    flux_buf, lift_ref, slots, sems,
):
    elems = main_ref.shape[0]
    width = elems // GROUPS
    small = [
        pltpu.make_async_copy(src, dst, sems.at[GROUPS + n])
        for n, (src, dst) in enumerate(
            [(flux_ref, flux_buf), (lift_hbm, lift_ref), (up_ref, slots.at[0]), (down_ref, slots.at[1])]
        )
    ]
    large = []
    for p in range(GROUPS):
        rows = pl.ds(p * width, width)
        large.append(pltpu.make_async_copy(inverse_ref.at[rows], main_ref.at[rows], sems.at[p]))
    for copy in small + large:
        copy.start()
    for copy in small:
        copy.wait()
    row = lax.broadcasted_iota(jnp.int32, (elems, 128), 0)
    for n, out in enumerate((up_out, down_out)):
        local = (slots[n] & (elems - 1)).astype(F32)
        out[...] = jnp.broadcast_to(local, (128, elems)).T - row.astype(F32)
    live_ref[...] = jnp.where(row < count_ref[0, 0], 1.0, 0.0)
    lane = lax.broadcasted_iota(jnp.int32, (elems, 128), 1)
    for d in range(4):
        lift_t = lift_ref[d].T
        both = jnp.concatenate([lift_t, lift_t], axis=1)
        none = jnp.zeros_like(both)
        weight = jnp.concatenate(
            [jnp.concatenate([both, none], axis=1), jnp.concatenate([none, both], axis=1)], axis=0
        )
        high, low = split(weight)
        high_ref[d] = jnp.concatenate([high, high], axis=0)
        low_ref[d] = low
        flux = flux_buf[:, d, :]
        flux = jnp.concatenate([flux, jnp.zeros((7, elems), F32)], axis=0).T
        for v in range(NVAR):
            for k in range(3):
                u = 2 * k
                first = jnp.broadcast_to(flux[:, 5 * u + v : 5 * u + v + 1], (elems, 128))
                if u + 1 < NVAR:
                    at = 5 * (u + 1) + v
                    second = jnp.broadcast_to(flux[:, at : at + 1], (elems, 128))
                else:
                    second = jnp.zeros((elems, 128), F32)
                mix_ref[d, v, :, 128 * k : 128 * k + 128] = jnp.where(lane < NB, first, second)
    for p in range(GROUPS):
        large[p].wait()

        @pl.loop(p * width // 4, (p + 1) * width // 4)
        def _(q):
            rem_ref[q] = jnp.concatenate([main_ref[4 * q + j, :, 256:320] for j in range(4)], axis=1)


def face_of(x, d, mix_ref, high_ref, low_ref):
    return couple(x, high_ref[d], low_ref[d], [mix_ref[d, v] for v in range(NVAR)])


def beside(shift_ref, left_ref, right_ref):
    elems = shift_ref.shape[0] - 16
    shift_ref[7:8, :] = left_ref[...]
    shift_ref[elems + 8 : elems + 9, :] = right_ref[...]
    return shift_ref[7 : elems + 7, :], shift_ref[9 : elems + 9, :]


def put_groups(fixed, refs):
    width = refs[0].shape[0]
    for p, ref in enumerate(refs):
        ref[...] = fixed[p * width : p * width + width]


def setup_kernel(
    rhs_ref, old_ref, next_ref, left_ref, right_ref, delta_ref, mix_ref, high_ref, low_ref, *refs
):
    fixed_refs, (source_ref, shift_ref) = refs[:GROUPS], refs[GROUPS:]
    elems = rhs_ref.shape[0]
    source = padded(rhs_ref[...])
    source_ref[...] = source
    shift_ref[8 : elems + 8, :] = padded(old_ref[...])
    before, after = beside(shift_ref, left_ref, right_ref)
    below = gathered(padded(next_ref[...]), delta_ref[...])
    fixed = source - face_of(below, 1, mix_ref, high_ref, low_ref)
    fixed = fixed - face_of(before, 2, mix_ref, high_ref, low_ref)
    put_groups(fixed - face_of(after, 3, mix_ref, high_ref, low_ref), fixed_refs)


def turn_kernel(source_ref, left_ref, right_ref, mix_ref, high_ref, low_ref, *refs):
    states, uppers = refs[:GROUPS], refs[GROUPS : 2 * GROUPS]
    fixed_refs, (shift_ref,) = refs[2 * GROUPS : 3 * GROUPS], refs[3 * GROUPS :]
    width = states[0].shape[0]
    for p in range(GROUPS):
        shift_ref[8 + p * width : 8 + p * width + width, :] = states[p][...]
    before, after = beside(shift_ref, left_ref, right_ref)
    fixed = source_ref[...] - jnp.concatenate([upper[...] for upper in uppers], axis=0)
    fixed = fixed - face_of(before, 2, mix_ref, high_ref, low_ref)
    put_groups(fixed - face_of(after, 3, mix_ref, high_ref, low_ref), fixed_refs)


def join_kernel(*refs):
    width = refs[0].shape[0]
    for n in range(2):
        for p in range(GROUPS):
            refs[2 * GROUPS + n][p * width : p * width + width, :] = refs[n * GROUPS + p][:, :320]


def step_kernel(
    layer, face, group, keep, flipped, first_layer,
    message_ref, main_ref, rem_ref, fixed_ref, mix_ref, high_ref, delta_ref, live_ref,
    token_ref, *refs,
):
    del token_ref
    count = 2 if keep else 1
    held_refs, new_refs, (body_ref,) = refs[:count], refs[count : 2 * count], refs[2 * count :]
    width = message_ref.shape[0]
    active = lax.axis_index("flow") == layer

    @pl.when(active)
    def _():
        base = group * width
        rows = pl.ds(base, width)
        if first_layer:
            inflow = jnp.zeros((width, WIDE), F32)
        else:
            mix = [mix_ref[face, v, rows, :] for v in range(NVAR)]
            inflow = couple(gathered(message_ref[...], delta_ref[rows, :]), high_ref[face], None, mix)
        if keep:
            new_refs[1][...] = inflow
        resid = fixed_ref[...] - inflow
        tail = resid[:, 256:]
        tail = tail + pltpu.roll(tail, 64, 1)
        row = lax.broadcasted_iota(jnp.int32, (width, 256), 0)
        lane = lax.broadcasted_iota(jnp.int32, (width, 256), 1)
        body_ref[:, :256] = resid[:, :256]
        body_ref[:, 256:] = jnp.where(row % 4 == lane // 64, jnp.concatenate([tail, tail], axis=1), 0.0)
        at = lax.broadcasted_iota(jnp.int32, (BLOCK, 320), 0)

        @pl.loop(0, width // BLOCK)
        def _(b):
            part = pl.ds(pl.multiple_of(b * BLOCK, BLOCK), BLOCK)
            both = body_ref[part, :].astype(BF16)
            first = base + b * BLOCK
            rest = jnp.zeros((BLOCK, 320), F32)
            solved = jnp.zeros((BLOCK, 320), F32)
            times = dot if flipped else dot_t
            for q in range(BLOCK // 4):
                rest = jnp.where(at // 4 == q, times(both[:, 256:], rem_ref[first // 4 + q]), rest)
                for e in range(4 * q, 4 * q + 4):
                    block = main_ref[first + e] if flipped else main_ref[first + e, :, :256]
                    solved = jnp.where(at == e, times(both[:, :256], block), solved)
            wide = padded(solved + rest)
            live = live_ref[pl.ds(pl.multiple_of(first, BLOCK), BLOCK), :]
            wide = wide * jnp.concatenate([live, live, live], axis=1)
            new_refs[0][part, :] = wide

    @pl.when(jnp.logical_not(active))
    def _():
        for held, new in zip(held_refs, new_refs):
            new[...] = held[...]


def flip_kernel(low, high, inverse_ref, token_ref, *refs):
    main_ref, rem_ref, done_ref = refs[-3:]
    place = lax.axis_index("flow")
    done_ref[...] = jnp.zeros_like(done_ref)

    @pl.when((place >= low) & (place < high))
    def _():
        @pl.loop(0, inverse_ref.shape[0] // 4)
        def _(q):
            for j in range(4):
                turned = inverse_ref[4 * q + j].T
                main_ref[4 * q + j] = turned[:256]
                rem_ref[q, 64 * j : 64 * j + 64, :] = turned[256:]


def flip_call(inverse, token, earlier, low, high):
    elems = inverse.shape[0]
    return pl.pallas_call(
        functools.partial(flip_kernel, low, high),
        out_shape=(
            jax.ShapeDtypeStruct((elems, 256, 320), BF16),
            jax.ShapeDtypeStruct((elems // 4, 256, 320), BF16),
            jax.ShapeDtypeStruct((8, 128), F32),
        ),
        in_specs=[VMEM_SPEC, ANY_SPEC] + [VMEM_SPEC] * len(earlier),
        out_specs=(VMEM_SPEC,) * 3,
        input_output_aliases={2 + n: n for n in range(len(earlier))},
        compiler_params=pltpu.CompilerParams(vmem_limit_bytes=STEP_VMEM),
        name="sweep_flip",
    )(inverse, token, *earlier)


def step_call(layer, face, group, keep, flipped, first_layer, width):
    body = functools.partial(step_kernel, layer, face, group, keep, flipped, first_layer)
    count = 2 if keep else 1
    cells = jax.ShapeDtypeStruct((width, WIDE), F32)
    return pl.pallas_call(
        body,
        out_shape=(cells,) * count,
        in_specs=[VMEM_SPEC] * 8 + [ANY_SPEC] + [VMEM_SPEC] * count,
        out_specs=(VMEM_SPEC,) * count,
        scratch_shapes=[pltpu.VMEM((width, 512), F32)],
        compiler_params=pltpu.CompilerParams(
            vmem_limit_bytes=STEP_VMEM
        ),
        cost_estimate=pl.CostEstimate(flops=width * 320 * 320 * 2, bytes_accessed=width * 320 * 320 * 2, transcendentals=0),
        name="sweep_step",
    )


def edge_rows(first, last):
    count = lax.axis_size("cross")
    right = [(i, i + 1) for i in range(count - 1)]
    left = [(i + 1, i) for i in range(count - 1)]
    return lax.ppermute(last, "cross", right), lax.ppermute(first, "cross", left)


def sweep(fixed, table, flips, delta, live, face, keep, route):
    width = fixed[0].shape[0]
    blank = jnp.zeros((width, WIDE), F32)
    messages = [blank] * GROUPS
    held = [(blank,) * (2 if keep else 1)] * GROUPS
    token = fixed[0]
    last = len(route) - 1
    for i, layer in enumerate(route):
        for p in ORDER:
            flipped = len(flips) == 2
            call = step_call(layer, face, p, keep, flipped, i == 0, width)
            main, rem, mix, high = table[:4]
            if flipped:
                main, rem = flips[1]
            new = call(messages[p], main, rem, fixed[p], mix, high, delta, live, token, *held[p])
            token = new[0]
            held[p] = tuple(new)
            if i < last:
                pairs = [(route[k], route[k + 1]) for k in range(i % SPAN, last, SPAN)]
                messages[p] = lax.ppermute(token, "flow", pairs)
        if keep and i == 0:
            *flip, token = flip_call(table[0], token, (), MIDDLE, len(route))
            flips.append(flip)
        if keep and i == MIDDLE + 1:
            *flip, token = flip_call(table[0], token, flips[0], 0, MIDDLE)
            flips.append(flip)
    return held


def per_device(
    right_side, old_state, block_inverse, flux_jacobian, face_lift, upstream, downstream, live_counts
):
    layers = lax.axis_size("flow")
    rhs = right_side[0]
    elems = rhs.shape[0]
    width = elems // GROUPS
    alive = jnp.arange(elems, dtype=jnp.int32)[:, None] < live_counts[0, 0]
    old = jnp.where(alive, old_state[0], 0.0)
    following = lax.ppermute(old, "flow", [(l + 1, l) for l in range(layers - 1)])
    edge = jnp.pad(old[:1], ((0, 0), (0, WIDE - 320))), jnp.pad(old[-1:], ((0, 0), (0, WIDE - 320)))
    left, right = edge_rows(*edge)
    flux = jnp.transpose(flux_jacobian[0], (2, 1, 0))
    shift = pltpu.VMEM((elems + 16, WIDE), F32)
    cells = jax.ShapeDtypeStruct((elems, WIDE), F32)
    group_cells = (jax.ShapeDtypeStruct((width, WIDE), F32),) * GROUPS
    prep = pltpu.CompilerParams(vmem_limit_bytes=PREP_VMEM)
    *table, up, down, live = pl.pallas_call(
        load_kernel,
        out_shape=(
            jax.ShapeDtypeStruct((elems, 320, 320), BF16),
            jax.ShapeDtypeStruct((elems // 4, 320, 256), BF16),
            jax.ShapeDtypeStruct((4, NVAR, elems, WIDE), F32),
            jax.ShapeDtypeStruct((4, 256, 256), BF16),
            jax.ShapeDtypeStruct((4, 128, 256), BF16),
        ) + (jax.ShapeDtypeStruct((elems, 128), F32),) * 3,
        in_specs=[pl.BlockSpec(memory_space=pltpu.SMEM)] + [HBM_SPEC] * 5,
        out_specs=(VMEM_SPEC,) * 8,
        scratch_shapes=[
            pltpu.VMEM((25, 4, elems), F32),
            pltpu.VMEM((4, NB, NB), F32),
            pltpu.VMEM((2, 1, elems), jnp.int32),
            pltpu.SemaphoreType.DMA((GROUPS + 4,)),
        ],
        compiler_params=pltpu.CompilerParams(vmem_limit_bytes=LOAD_VMEM),
        name="sweep_load",
    )(live_counts, *[
        pltpu.with_memory_space_constraint(x, pltpu.HBM)
        for x in (block_inverse[0], flux, face_lift, upstream, downstream)
    ])
    mixing = table[2:]
    *fixed, source = pl.pallas_call(
        setup_kernel,
        out_shape=group_cells + (cells,),
        in_specs=[VMEM_SPEC] * 9,
        out_specs=(VMEM_SPEC,) * (GROUPS + 1),
        scratch_shapes=[shift],
        compiler_params=prep,
        name="sweep_setup",
    )(rhs, old, following, left, right, down, *mixing)
    flips = []
    held = sweep(fixed, table, flips, up, live, 0, True, list(range(layers)))
    states = [state for state, _ in held]
    uppers = [upper for _, upper in held]
    left, right = edge_rows(states[0][:1], states[-1][-1:])
    fixed = pl.pallas_call(
        turn_kernel,
        out_shape=group_cells,
        in_specs=[VMEM_SPEC] * (6 + 2 * GROUPS),
        out_specs=(VMEM_SPEC,) * GROUPS,
        scratch_shapes=[shift],
        compiler_params=prep,
        name="sweep_turn",
    )(source, left, right, *mixing, *states, *uppers)
    held = sweep(fixed, table, flips, down, live, 1, False, list(reversed(range(layers))))
    half, full = pl.pallas_call(
        join_kernel,
        out_shape=(jax.ShapeDtypeStruct((elems, 320), F32),) * 2,
        in_specs=[VMEM_SPEC] * (2 * GROUPS),
        out_specs=(VMEM_SPEC,) * 2,
        compiler_params=pltpu.CompilerParams(vmem_limit_bytes=STEP_VMEM),
        name="sweep_join",
    )(*states, *[state for state, in held])
    return half[None], full[None]


def solution(mesh):
    in_specs = (
        P("flow", "cross", None),
        P("flow", "cross", None),
        P("flow", "cross", None, None),
        P("flow", "cross", None, None),
        P(),
        P("flow", "cross"),
        P("flow", "cross"),
        P("flow", "cross"),
    )
    out_specs = (P("flow", "cross", None), P("flow", "cross", None))
    return jax.shard_map(
        per_device, mesh=mesh, in_specs=in_specs, out_specs=out_specs, check_vma=False
    )
```
